256 devices in a mesh: section: 16 (over x_hi, z), lane: 16 (over y, x_lo, core).
Axes of the slice: x: 4 (x_hi: 2, x_lo: 2; x = x_hi * 2 + x_lo), y: 4, z: 8, core: 2. Of those that a mesh axis runs over, the one named last changes fastest.
Arguments:
- value_weight: float32 [16, 1024, 256], P('section', 'lane'), may hold values from -0.1875 to 0.1875
- out_weight: float32 [16, 2048, 1024], P('section', 'lane'), may hold values from -0.125 to 0.125
- value_moment: float32 [16, 1024, 256], P('section', 'lane'), may hold values from -6 to 6
- out_moment: float32 [16, 2048, 1024], P('section', 'lane'), may hold values from -6 to 6
- inputs_saved: bfloat16 [2, 2, 16, 2048, 1024], P(None, None, 'section', 'lane'), may hold values from -6 to 6
- queries_saved: bfloat16 [2, 2, 16, 2048, 2048], P(None, None, 'section', 'lane'), may hold values from -100 to 100
- keys_saved: bfloat16 [2, 2, 16, 2048, 256], P(None, None, 'section', 'lane'), may hold values from -5 to 5
- grad_now: bfloat16 [2, 16, 2048, 1024], P(None, 'section', 'lane'), may hold values from -6 to 6
- grad_new: bfloat16 [2, 2048, 1024], P(None, 'lane'), may hold values from -6 to 6
- bound_now: int32 [2, 16, 16], P(None, None, 'lane'), may hold values from 1 to 127
- bound_new: int32 [2, 16], P(None, 'lane'), may hold values from 1 to 127
Outputs:
- grad_inputs: bfloat16 [2, 2, 16, 2048, 1024], P(None, None, 'section', 'lane')
- grad_queries: bfloat16 [2, 2, 16, 2048, 2048], P(None, None, 'section', 'lane')
- grad_keys: bfloat16 [2, 2, 16, 2048, 256], P(None, None, 'section', 'lane')
- value_weight_new: float32 [16, 1024, 256], P('section', 'lane')
- out_weight_new: float32 [16, 2048, 1024], P('section', 'lane')
- value_moment_new: float32 [16, 1024, 256], P('section', 'lane')
- out_moment_new: float32 [16, 2048, 1024], P('section', 'lane')
The draws below stay inside these ranges and needn't reach their ends.
All inputs are finite; a program needn't handle non-finite values.
Results may differ from the reference program's by a relative error of at most 0.018.
Values may be sent and summed in bfloat16 or wider, within the bound.
A program may use at most 128 MiB of HBM per device.

```python
import math
import jax
import jax.numpy as jnp
from jax import lax

D = 1024
QUERY_HEAD_COUNT = 16
KEY_VALUE_HEADS = 2
HEAD_SIZE = 128
TOK = 128
MICRO_TICKS = 2
QW = 2048
KVW = 256
RELAY_SECTIONS = 16
LANES = 16
N_LANE = 16


def paired_draw(key):
    base = jax.random.fold_in(key, 7)
    first_random_key, second_random_key = jax.random.split(base, 2)
    query_group = QUERY_HEAD_COUNT // KEY_VALUE_HEADS
    token_rows = LANES * TOK
    key_rows = jnp.clip(jax.random.normal(first_random_key, (2, MICRO_TICKS, RELAY_SECTIONS, token_rows, KEY_VALUE_HEADS, HEAD_SIZE), jnp.float32), -4.0, 4.0)
    query_rows = jnp.clip(jax.random.normal(second_random_key, (2, MICRO_TICKS, RELAY_SECTIONS, token_rows, KEY_VALUE_HEADS, query_group, HEAD_SIZE), jnp.float32), -4.0, 4.0)
    return (query_rows.reshape(2, MICRO_TICKS, RELAY_SECTIONS, token_rows, QW), key_rows.reshape(2, MICRO_TICKS, RELAY_SECTIONS, token_rows, KVW))


def draw_queries_saved(key, part):
    return paired_draw(key)[0].astype(jnp.bfloat16)


def draw_keys_saved(key, part):
    return paired_draw(key)[1].astype(jnp.bfloat16)


def set_ends(values, rng, smallest, high):
    longest = values.shape.index(max(values.shape))
    spots = []
    for shift in (0, 1):
        where = [jax.random.randint(jax.random.fold_in(rng, axis), (), 0, length) for axis, length in enumerate(values.shape)]
        where[longest] = (where[longest] + shift) % values.shape[longest]
        spots.append(tuple(where))
    return values.at[spots[0]].set(smallest).at[spots[1]].set(high)


def level_of(rng, dims, cuts, least, high):
    gain, own = 1.0, jax.random.fold_in(rng, 6)
    for dim, shards_of in cuts:
        draws = jnp.exp(jax.random.uniform(jax.random.fold_in(own, dim), (shards_of,), jnp.float32, least / len(cuts), high / len(cuts)))
        gain = gain * jnp.repeat(draws, dims[dim] // shards_of).reshape([-1 if axis == dim else 1 for axis in range(len(dims))])
    return gain


def bell_draw(rng, extent, scale, reach, cuts=(), dtype=jnp.bfloat16):
    result = scale * jax.random.normal(rng, extent, jnp.float32)
    if cuts:
        result = result * level_of(rng, extent, cuts, -0.22, 0.18)
    return jnp.clip(result, -reach, reach).astype(dtype)


def setup_inputs(seed: int = 0) -> dict:
    splits = jax.random.split(jax.random.key(seed), 12)
    return {
        "value_weight": bell_draw(splits[0], (RELAY_SECTIONS, D, KVW), D ** -0.5, 0.1875, ((0, 16), (1, 16)), jnp.float32),
        "out_weight": bell_draw(splits[1], (RELAY_SECTIONS, QW, D), QW ** -0.5, 0.125, ((0, 16), (1, 16)), jnp.float32),
        "value_moment": bell_draw(splits[2], (RELAY_SECTIONS, D, KVW), 1.0, 6.0, ((0, 16), (1, 16)), jnp.float32),
        "out_moment": bell_draw(splits[3], (RELAY_SECTIONS, QW, D), 1.0, 6.0, ((0, 16), (1, 16)), jnp.float32),
        "inputs_saved": bell_draw(splits[4], (2, MICRO_TICKS, RELAY_SECTIONS, LANES * TOK, D), 1.0, 6.0, ((2, 16), (3, 16))),
        "queries_saved": draw_queries_saved(jax.random.fold_in(splits[11], 71), 0),
        "keys_saved": draw_keys_saved(jax.random.fold_in(splits[11], 71), 0),
        "grad_now": bell_draw(splits[7], (2, RELAY_SECTIONS, LANES * TOK, D), 1.0, 6.0, ((1, 16), (2, 16))),
        "grad_new": bell_draw(splits[8], (2, LANES * TOK, D), 1.0, 6.0, ((1, 16),)),
        "bound_now": set_ends(jax.random.randint(splits[9], (2, RELAY_SECTIONS, LANES), 1, TOK), jax.random.fold_in(splits[9], 1), 1, TOK - 1).astype(jnp.int32),
        "bound_new": set_ends(jax.random.randint(splits[10], (2, LANES), 1, TOK), jax.random.fold_in(splits[10], 1), 1, TOK - 1).astype(jnp.int32),
    }


decay_rate = 0.9
learn_rate = 0.01

def lowered(array):
    return lax.optimization_barrier(array.astype(jnp.bfloat16)).astype(jnp.float32)

def attend(inputs, query_rows, key_rows, cotangent, bounds, w_value, w_out, full):
    relay_lanes, token_rows, _ = inputs.shape
    query_group = QUERY_HEAD_COUNT // KEY_VALUE_HEADS
    scale_factor = 1.0 / math.sqrt(HEAD_SIZE)
    value_matrix = jnp.einsum('ltd,dc->ltc', inputs.astype(jnp.float32), w_value.astype(jnp.float32)).astype(jnp.bfloat16)
    heads_of_query = query_rows.astype(jnp.float32).reshape(relay_lanes, token_rows, KEY_VALUE_HEADS, query_group, HEAD_SIZE)
    heads_of_key = key_rows.astype(jnp.float32).reshape(relay_lanes, token_rows, KEY_VALUE_HEADS, HEAD_SIZE)
    heads_of_value = value_matrix.astype(jnp.float32).reshape(relay_lanes, token_rows, KEY_VALUE_HEADS, HEAD_SIZE)
    scores = jnp.einsum('lihgd,ljhd->lhgij', heads_of_query, heads_of_key) * scale_factor
    places = jnp.arange(token_rows)
    earlier = places[None, :] <= places[:, None]
    second = places[None, :] >= bounds[:, None]
    same_doc = second[:, :, None] == second[:, None, :]
    allowed = (earlier[None] & same_doc)[:, None, None]
    scores = jnp.where(allowed, scores, -1e+30)
    top_score = lax.optimization_barrier(jnp.max(scores, axis=-1, keepdims=True))
    expo = jnp.exp(scores - top_score)
    probs = expo / lax.optimization_barrier(jnp.sum(expo, axis=-1, keepdims=True))
    probs_low = lowered(probs)
    attended = jnp.einsum('lhgij,ljhd->lihgd', probs_low, heads_of_value).astype(jnp.bfloat16).reshape(relay_lanes, token_rows, QW)
    attended_gradient = jnp.einsum('ltd,cd->ltc', cotangent.astype(jnp.float32), w_out.astype(jnp.float32)).astype(jnp.bfloat16)
    head_gradient = attended_gradient.astype(jnp.float32).reshape(relay_lanes, token_rows, KEY_VALUE_HEADS, query_group, HEAD_SIZE)
    grad_values = jnp.einsum('lhgij,lihgd->ljhd', probs_low, head_gradient).astype(jnp.bfloat16).reshape(relay_lanes, token_rows, KVW)
    grad_inputs = (cotangent.astype(jnp.float32) + jnp.einsum('ltc,dc->ltd', grad_values.astype(jnp.float32), w_value.astype(jnp.float32))).astype(jnp.bfloat16)
    if not full:
        return grad_inputs
    grad_probs = jnp.einsum('lihgd,ljhd->lhgij', head_gradient, heads_of_value)
    delta = lax.optimization_barrier(jnp.sum(probs * grad_probs, axis=-1, keepdims=True))
    grad_scores = lowered(probs * (grad_probs - delta) * scale_factor)
    grad_queries = jnp.einsum('lhgij,ljhd->lihgd', grad_scores, heads_of_key).astype(jnp.bfloat16).reshape(relay_lanes, token_rows, QW)
    grad_keys = jnp.einsum('lhgij,lihgd->ljhd', grad_scores, heads_of_query).astype(jnp.bfloat16).reshape(relay_lanes, token_rows, KVW)
    grad_wvalue = jnp.einsum('ltd,ltc->ldc', inputs.astype(jnp.float32), grad_values.astype(jnp.float32))
    grad_wout = jnp.einsum('ltc,ltd->lcd', attended.astype(jnp.float32), cotangent.astype(jnp.float32))
    return (grad_inputs, grad_queries, grad_keys, grad_wvalue, grad_wout)

def reference(value_weight, out_weight, value_moment, out_moment, inputs_saved, queries_saved, keys_saved, grad_now, grad_new, bound_now, bound_new):
    sections = value_weight.shape[0]
    relay_lanes = N_LANE
    value_low = value_weight.astype(jnp.bfloat16)
    out_low = out_weight.astype(jnp.bfloat16)

    def split_rows(array):
        return array.reshape(array.shape[:-2] + (relay_lanes, TOK, array.shape[-1]))
    inputs_all = split_rows(inputs_saved)
    queries_all = split_rows(queries_saved)
    keys_all = split_rows(keys_saved)
    grads_first = split_rows(grad_now)
    grads_fresh = split_rows(grad_new)
    indices = jnp.arange(sections)
    handed = []
    for direction in range(2):

        def tick_zero(place, direction=direction):
            section = place if direction == 0 else sections - 1 - place
            return attend(inputs_all[direction, 0, place], queries_all[direction, 0, place], keys_all[direction, 0, place], grads_first[direction, place], bound_now[direction, place], value_low[section], out_low[section], False)
        handed.append(lax.map(tick_zero, indices))
    second_grads = [jnp.concatenate([handed[0][1:], grads_fresh[0][None]], axis=0), jnp.concatenate([grads_fresh[1][None], handed[1][:-1]], axis=0)]
    second_bounds = [jnp.concatenate([bound_now[0, 1:], bound_new[0][None]], axis=0), jnp.concatenate([bound_new[1][None], bound_now[1, :-1]], axis=0)]
    results = []
    for direction in range(2):

        def both_ticks(place, direction=direction):
            section = place if direction == 0 else sections - 1 - place
            first = attend(inputs_all[direction, 0, place], queries_all[direction, 0, place], keys_all[direction, 0, place], grads_first[direction, place], bound_now[direction, place], value_low[section], out_low[section], True)
            later = attend(inputs_all[direction, 1, place], queries_all[direction, 1, place], keys_all[direction, 1, place], second_grads[direction][place], second_bounds[direction][place], value_low[section], out_low[section], True)
            part_value = lax.optimization_barrier(jnp.sum(lowered(first[3] + later[3]), axis=0))
            part_out = lax.optimization_barrier(jnp.sum(lowered(first[4] + later[4]), axis=0))
            return ((first[0], later[0]), (first[1], later[1]), (first[2], later[2]), part_value, part_out)
        results.append(lax.map(both_ticks, indices))

    def assemble(slot, width):
        stacked = jnp.stack([jnp.stack([results[r][slot][0], results[r][slot][1]]) for r in range(2)])
        return stacked.reshape(2, MICRO_TICKS, sections, relay_lanes * TOK, width)
    grad_inputs = assemble(0, D)
    grad_queries = assemble(1, QW)
    grad_keys = assemble(2, KVW)
    grad_value = (results[0][3] + results[1][3][::-1]) / relay_lanes
    grad_out = (results[0][4] + results[1][4][::-1]) / relay_lanes
    value_moment_new = decay_rate * value_moment + grad_value
    out_moment_new = decay_rate * out_moment + grad_out
    value_weight_new = value_weight - learn_rate * value_moment_new
    out_weight_new = out_weight - learn_rate * out_moment_new
    return (grad_inputs, grad_queries, grad_keys, value_weight_new, out_weight_new, value_moment_new, out_moment_new)
```

```python
import functools
import math

import jax
import jax.numpy as jnp
from jax import lax
from jax.experimental import pallas as pl
from jax.experimental.pallas import tpu as pltpu
from jax.sharding import PartitionSpec as P

TOK = 128
D = 1024
QW = 2048
KVW = 256
HS = 128
HEADS = 16
GROUP = 8
LANES = 16
ROWS = 144
CUT = 80

decay_rate = 0.9
learn_rate = 0.01
MESH = pl.DeviceIdType.MESH
bf16 = jnp.bfloat16
f32 = jnp.float32

PLACES = ((2, 1), (1, 1), (3, 1), (2, 0), (1, 0), (3, 0), (0, 1), (0, 0))


def dot(a, b, dims):
    return lax.dot_general(a, b, (dims, ((), ())), preferred_element_type=f32)


def kernel(
    sections,
    bn, bw, wv_in, wo_in, x_hbm, q_hbm, k_hbm, gnow_hbm, gnew_hbm,
    gi_hbm, dq_hbm, dk_hbm, gsum_ref,
    wb, wvs, xs, qs, ks, gs, gnews, pr, vs, at, ga, dvs, gis, dqs, dks, rx,
    dwv, pc, po, rc, rn, msend, mrecv, fin, maskb,
    ld_sem, st_sem, ag_send, ag_recv, rs_send, rs_recv, ms_send, ms_recv, nb_send, nb_recv,
):
    s = lax.axis_index("section")
    l = lax.axis_index("lane")
    y = l // 4
    x = (l // 2) % 2
    c = l % 2
    scale = 1.0 / math.sqrt(HS)

    def lane(dy, dx, dc):
        yy = (y + dy) % 4
        xx = (x + dx) % 2
        cc = (c + dc) % 2
        return yy * 4 + xx * 2 + cc

    def slot(q, dy, dx, dc):
        return lane(dy, dx + q, dc)

    xp = (s, lane(0, 1, 0))
    yp = (s, lane(1, 0, 0))
    ym = (s, lane(3, 0, 0))
    cp = (s, lane(0, 0, 1))
    mir = (sections - 1 - s, lane(0, 1, 0))
    before = ((s + sections - 1) % sections, l)
    after = ((s + 1) % sections, l)

    loads = [
        pltpu.make_async_copy(k_hbm, ks, ld_sem.at[0]),
        pltpu.make_async_copy(q_hbm, qs, ld_sem.at[1]),
        pltpu.make_async_copy(x_hbm, xs, ld_sem.at[2]),
        pltpu.make_async_copy(gnow_hbm, gs.at[:, 0], ld_sem.at[3]),
        pltpu.make_async_copy(gnew_hbm, gnews, ld_sem.at[4]),
    ]
    for cpy in loads:
        cpy.start()

    barrier = pltpu.get_barrier_semaphore()
    peers = (xp, yp, ym, cp, mir, before, after)
    for p in peers:
        pl.semaphore_signal(barrier, inc=1, device_id=p, device_id_type=MESH)
    wb[0, l, :TOK, :] = wo_in[...].astype(bf16)
    for j in range(4):
        wb[0, l, TOK:, j * KVW : (j + 1) * KVW] = wv_in[16 * j : 16 * (j + 1), :].astype(bf16)
    pl.semaphore_wait(barrier, len(peers))

    sent = []

    def send(src, dst, ssem, rsem, dev):
        cpy = pltpu.make_async_remote_copy(
            src_ref=src, dst_ref=dst, send_sem=ssem, recv_sem=rsem, device_id=dev, device_id_type=MESH
        )
        cpy.start()
        sent.append(cpy)

    def arrived(dst, sem):
        pltpu.make_async_copy(dst, dst, sem).wait()

    OWN, X, A, B, OPP, AX, BX, OX = range(8)
    where_is = {
        OWN: (0, 0), X: (0, 1), A: (3, 0), B: (1, 0), OPP: (2, 0), AX: (3, 1), BX: (1, 1), OX: (2, 1),
    }

    def block(q, kind, core=0):
        return wb.at[q, slot(q, *where_is[kind], core)]

    def ag_send_block(q, n, kind, to, rkind, rows=None):
        ref = block(q, kind)
        if rows is not None:
            ref = ref.at[pl.ds(*rows), :]
        send(ref, ref, ag_send.at[q, n], ag_recv.at[q, rkind], to)

    def ag_core(q, kind):
        ref = block(q, kind)
        send(ref, ref, ag_send.at[q, 8 + kind], ag_recv.at[q, 8 + kind], cp)

    def ag_start(q):
        ag_send_block(q, 0, OWN, yp, 1)
        ag_send_block(q, 1, OWN, ym, 2)
        ag_send_block(q, 2, OWN, xp, 0)
        ag_core(q, OWN)

    def ag_step1(q):
        arrived(block(q, A), ag_recv.at[q, 1])
        ag_send_block(q, 3, A, yp, 3, (0, CUT))
        arrived(block(q, B), ag_recv.at[q, 2])
        ag_send_block(q, 4, B, ym, 4, (CUT, ROWS - CUT))
        arrived(block(q, X), ag_recv.at[q, 0])
        ag_send_block(q, 5, X, yp, 5)
        ag_send_block(q, 6, X, ym, 6)
        ag_core(q, A)
        ag_core(q, B)
        ag_core(q, X)

    def ag_step2(q):
        ref = block(q, OPP)
        arrived(ref.at[pl.ds(0, CUT), :], ag_recv.at[q, 3])
        arrived(ref.at[pl.ds(CUT, ROWS - CUT), :], ag_recv.at[q, 4])
        ag_send_block(q, 7, OPP, xp, 7)
        ag_core(q, OPP)

    def ag_step3(q):
        arrived(block(q, AX), ag_recv.at[q, 5])
        ag_core(q, AX)
        arrived(block(q, BX), ag_recv.at[q, 6])
        ag_core(q, BX)
        arrived(block(q, OX), ag_recv.at[q, 7])
        ag_core(q, OX)

    def ag_finish(q):
        for kind in range(8):
            arrived(block(q, kind, 1), ag_recv.at[q, 8 + kind])

        @pl.loop(0, LANES)
        def _(h):
            for j in range(4):
                at_row = pl.multiple_of(h * 64 + 16 * j, 16)
                wvs[q, pl.ds(at_row, 16), :] = wb[q, h, TOK:, j * KVW : (j + 1) * KVW]

    def softmax(q, t):
        here = bn[q, s]
        if t == 0:
            bound = here
        elif q == 0:
            bound = jnp.where(s == sections - 1, bw[0], bn[0, jnp.minimum(s + 1, sections - 1)])
        else:
            bound = jnp.where(s == 0, bw[1], bn[1, jnp.maximum(s - 1, 0)])
        row = lax.broadcasted_iota(jnp.int32, (TOK, TOK), 0)
        col = lax.broadcasted_iota(jnp.int32, (TOK, TOK), 1)
        seen = (col <= row) & ((col >= bound) | (row < bound))
        maskb[...] = jnp.where(seen, 0.0, -1e30).astype(f32)
        for g in range(2):
            kg = ks[q, t, :, g * HS : (g + 1) * HS]

            @pl.loop(0, GROUP // 2)
            def _(n):
                for u in range(2):
                    h = g * GROUP + n * 2 + u
                    qh = qs[q, t, :, pl.ds(pl.multiple_of(h * HS, HS), HS)]
                    sc = dot(qh, kg, ((1,), (1,))) * scale + maskb[...]
                    e = jnp.exp(sc - jnp.max(sc, axis=-1, keepdims=True))
                    pr[q, t, h] = e * (1.0 / jnp.sum(e, axis=-1, keepdims=True))

    def values(q):
        for t in range(2):
            vs[q, t] = dot(xs[q, t], wvs[q], ((1,), (0,))).astype(bf16)

    def attended(q, t):
        for g in range(2):
            vg = vs[q, t, :, g * HS : (g + 1) * HS]

            @pl.loop(0, GROUP // 2)
            def _(n):
                for u in range(2):
                    h = g * GROUP + n * 2 + u
                    at[q, h, t * TOK : (t + 1) * TOK, :] = dot(pr[q, t, h].astype(bf16), vg, ((1,), (0,))).astype(bf16)

    def tick(q, t):
        @pl.loop(0, HEADS // 2)
        def _(n):
            w2 = jnp.concatenate([wb[q, 2 * n, :TOK, :], wb[q, 2 * n + 1, :TOK, :]], axis=0)
            r = dot(gs[q, t], w2, ((1,), (1,))).astype(bf16)
            ga[q, t, 2 * n] = r[:, :HS]
            ga[q, t, 2 * n + 1] = r[:, HS:]

        for g in range(2):
            p8 = pr[q, t, g * GROUP : (g + 1) * GROUP].astype(bf16).reshape(GROUP * TOK, TOK)
            g8 = ga[q, t, g * GROUP : (g + 1) * GROUP].reshape(GROUP * TOK, HS)
            dvs[q, t, :, g * HS : (g + 1) * HS] = dot(p8, g8, ((0,), (0,))).astype(bf16)
        for n in range(4):
            cols = slice(n * 256, (n + 1) * 256)
            add = dot(dvs[q, t], wvs[q, cols, :], ((1,), (1,)))
            gis[q, t, :, cols] = (gs[q, t, :, cols].astype(f32) + add).astype(bf16)

    def send_on(q):
        send(gis.at[q, 0], rx.at[q], nb_send.at[q], nb_recv.at[q], before if q == 0 else after)

    def take(q):
        arrived(rx.at[q], nb_recv.at[q])
        at_end = s == (sections - 1 if q == 0 else 0)
        gs[q, 1] = jnp.where(at_end, gnews[q], rx[q])

    def score_grads(q, t):
        for g in range(2):
            kg = ks[q, t, :, g * HS : (g + 1) * HS]
            vg = vs[q, t, :, g * HS : (g + 1) * HS]

            def body(n, acc):
                for u in range(2):
                    h = g * GROUP + n * 2 + u
                    at_col = pl.ds(pl.multiple_of(h * HS, HS), HS)
                    gp = dot(ga[q, t, h], vg, ((1,), (1,)))
                    p = pr[q, t, h]
                    delta = jnp.sum(p * gp, axis=-1, keepdims=True)
                    ds = (p * (gp - delta) * scale).astype(bf16)
                    dqs[q, t, :, at_col] = dot(ds, kg, ((1,), (0,))).astype(bf16)
                    acc = acc + dot(ds, qs[q, t, :, at_col], ((0,), (0,)))
                return acc

            acc = lax.fori_loop(0, GROUP // 2, body, jnp.zeros((TOK, HS), f32))
            dks[q, t, :, g * HS : (g + 1) * HS] = acc.astype(bf16)

    stores = []

    def store(src, dst):
        cpy = pltpu.make_async_copy(src, dst, st_sem.at[len(stores)])
        cpy.start()
        stores.append(cpy)

    def store_scores(q, t):
        store(dqs.at[q, t], dq_hbm.at[q, t])
        store(dks.at[q, t], dk_hbm.at[q, t])

    def rs_partials(q):
        xt = xs[q].reshape(2 * TOK, D)
        dv = dvs[q].reshape(2 * TOK, KVW)
        for n in range(4):
            dwv[q, n * 256 : (n + 1) * 256, :] = dot(xt[:, n * 256 : (n + 1) * 256], dv, ((0,), (0,))).astype(bf16)

        def one(ref, i, dc):
            dy, dx = PLACES[i]
            r = slot(q, dy, dx, dc)
            a = at[q, r]
            for n in range(2):
                cols = slice(n * 512, (n + 1) * 512)
                gg = gs[q, :, :, cols].reshape(2 * TOK, 512)
                ref[q, i, :TOK, cols] = dot(a, gg, ((0,), (0,))).astype(bf16)
            for j in range(4):
                at_row = pl.multiple_of(r * 64 + 16 * j, 16)
                ref[q, i, TOK:, j * KVW : (j + 1) * KVW] = dwv[q, pl.ds(at_row, 16), :]

        for i in range(8):
            one(pc, i, 1)
            send(pc.at[q, i], rc.at[q, i], rs_send.at[q, 8 + i], rs_recv.at[q, 8 + i], cp)
        for i in range(8):
            one(po, i, 0)

    R1, R2A, R2B, R3A, R3B, R4A, R4B, R5 = range(8)

    def plus(q, i, more, rows=slice(None)):
        total = po[q, i, rows, :].astype(f32)
        for n in more:
            total = total + (rn[q, n, rows, :] if n < 8 else rc[q, n - 8, rows, :]).astype(f32)
        return total

    def add_in(q, i, more, rows=slice(None)):
        po[q, i, rows, :] = plus(q, i, more, rows).astype(bf16)

    def rs_core(q, i):
        arrived(rc.at[q, i], rs_recv.at[q, 8 + i])

    def rs_hop(q, n, i, to, rows=None):
        src, dst = po.at[q, i], rn.at[q, n]
        if rows is not None:
            src, dst = src.at[pl.ds(*rows), :], dst.at[pl.ds(*rows), :]
        send(src, dst, rs_send.at[q, n], rs_recv.at[q, n], to)

    def rs_got(q, n, rows=None):
        dst = rn.at[q, n]
        if rows is not None:
            dst = dst.at[pl.ds(*rows), :]
        arrived(dst, rs_recv.at[q, n])

    def rs_a(q):
        for i, n, to in ((0, R1, xp), (1, R2A, yp), (2, R2B, ym)):
            rs_core(q, i)
            add_in(q, i, (8 + i,))
            rs_hop(q, n, i, to)

    def rs_b(q):
        rs_core(q, 3)
        rs_got(q, R1)
        add_in(q, 3, (8 + 3, R1))
        rs_hop(q, R3A, 3, yp, (0, CUT))
        rs_hop(q, R3B, 3, ym, (CUT, ROWS - CUT))
        rs_core(q, 6)
        rs_got(q, R2A)
        rs_got(q, R2B)
        add_in(q, 6, (8 + 6, R2A, R2B))
        rs_hop(q, R5, 6, xp)

    def rs_c(q):
        rs_core(q, 4)
        rs_got(q, R3A, (0, CUT))
        add_in(q, 4, (8 + 4, R3A), slice(0, CUT))
        add_in(q, 4, (8 + 4,), slice(CUT, ROWS))
        rs_hop(q, R4A, 4, yp)
        rs_core(q, 5)
        rs_got(q, R3B, (CUT, ROWS - CUT))
        add_in(q, 5, (8 + 5, R3B), slice(CUT, ROWS))
        add_in(q, 5, (8 + 5,), slice(0, CUT))
        rs_hop(q, R4B, 5, ym)

    def rs_final(q):
        rs_core(q, 7)
        rs_got(q, R4A)
        rs_got(q, R4B)
        rs_got(q, R5)
        total = plus(q, 7, (8 + 7, R4A, R4B, R5))
        if q == 0:
            fin[...] = total
        else:
            msend[...] = total.astype(bf16)
            send(msend, mrecv, ms_send.at[1], ms_recv.at[1], mir)

    own = block(0, OWN)
    send(own, wb.at[1, l], ms_send.at[0], ms_recv.at[0], mir)
    ag_start(0)
    loads[0].wait()
    loads[1].wait()
    softmax(0, 0)
    ag_step1(0)
    softmax(0, 1)
    ag_step2(0)
    softmax(1, 0)
    arrived(block(1, OWN), ms_recv.at[0])
    ag_start(1)
    ag_step3(0)
    loads[2].wait()
    loads[3].wait()
    loads[4].wait()
    ag_finish(0)
    values(0)
    tick(0, 0)
    send_on(0)
    store(gis.at[0, 0], gi_hbm.at[0, 0])
    ag_step1(1)
    attended(0, 0)
    attended(0, 1)
    ag_step2(1)
    softmax(1, 1)
    take(0)
    tick(0, 1)
    store(gis.at[0, 1], gi_hbm.at[0, 1])
    ag_step3(1)
    rs_partials(0)
    ag_finish(1)
    values(1)
    tick(1, 0)
    send_on(1)
    store(gis.at[1, 0], gi_hbm.at[1, 0])
    rs_a(0)
    attended(1, 0)
    attended(1, 1)
    rs_b(0)
    take(1)
    tick(1, 1)
    store(gis.at[1, 1], gi_hbm.at[1, 1])
    rs_c(0)
    rs_partials(1)
    rs_a(1)
    rs_final(0)
    score_grads(1, 0)
    store_scores(1, 0)
    rs_b(1)
    score_grads(1, 1)
    store_scores(1, 1)
    rs_c(1)
    score_grads(0, 0)
    store_scores(0, 0)
    rs_final(1)
    score_grads(0, 1)
    store_scores(0, 1)
    arrived(mrecv, ms_recv.at[1])
    gsum_ref[...] = (fin[...] + mrecv[...].astype(f32)) / LANES
    for cpy in stores:
        cpy.wait()
    for cpy in sent:
        cpy.wait_send()


def shards(
    value_weight, out_weight, value_moment, out_moment, inputs_saved, queries_saved, keys_saved,
    grad_now, grad_new, bound_now, bound_new,
):
    sections = lax.axis_size("section")
    hbm = pl.BlockSpec(memory_space=pl.ANY)
    vmem = pl.BlockSpec(memory_space=pltpu.VMEM)
    smem = pl.BlockSpec(memory_space=pltpu.SMEM)
    dma = pltpu.SemaphoreType.DMA
    gi, dq, dk, gsum = pl.pallas_call(
        functools.partial(kernel, sections),
        out_shape=(
            jax.ShapeDtypeStruct((2, 2, TOK, D), bf16),
            jax.ShapeDtypeStruct((2, 2, TOK, QW), bf16),
            jax.ShapeDtypeStruct((2, 2, TOK, KVW), bf16),
            jax.ShapeDtypeStruct((ROWS, D), f32),
        ),
        in_specs=[smem, smem, vmem, vmem, hbm, hbm, hbm, hbm, hbm],
        out_specs=(hbm, hbm, hbm, vmem),
        scratch_shapes=[
            pltpu.VMEM((2, LANES, ROWS, D), bf16),
            pltpu.VMEM((2, D, KVW), bf16),
            pltpu.VMEM((2, 2, TOK, D), bf16),
            pltpu.VMEM((2, 2, TOK, QW), bf16),
            pltpu.VMEM((2, 2, TOK, KVW), bf16),
            pltpu.VMEM((2, 2, TOK, D), bf16),
            pltpu.VMEM((2, TOK, D), bf16),
            pltpu.VMEM((2, 2, HEADS, TOK, TOK), f32),
            pltpu.VMEM((2, 2, TOK, KVW), bf16),
            pltpu.VMEM((2, HEADS, 2 * TOK, HS), bf16),
            pltpu.VMEM((2, 2, HEADS, TOK, HS), bf16),
            pltpu.VMEM((2, 2, TOK, KVW), bf16),
            pltpu.VMEM((2, 2, TOK, D), bf16),
            pltpu.VMEM((2, 2, TOK, QW), bf16),
            pltpu.VMEM((2, 2, TOK, KVW), bf16),
            pltpu.VMEM((2, TOK, D), bf16),
            pltpu.VMEM((2, D, KVW), bf16),
            pltpu.VMEM((2, 8, ROWS, D), bf16),
            pltpu.VMEM((2, 8, ROWS, D), bf16),
            pltpu.VMEM((2, 8, ROWS, D), bf16),
            pltpu.VMEM((2, 8, ROWS, D), bf16),
            pltpu.VMEM((ROWS, D), bf16),
            pltpu.VMEM((ROWS, D), bf16),
            pltpu.VMEM((ROWS, D), f32),
            pltpu.VMEM((TOK, TOK), f32),
            dma((5,)),
            dma((12,)),
            dma((2, 16)),
            dma((2, 16)),
            dma((2, 16)),
            dma((2, 16)),
            dma((2,)),
            dma((2,)),
            dma((2,)),
            dma((2,)),
        ],
        compiler_params=pltpu.CompilerParams(
            collective_id=0, has_side_effects=True, vmem_limit_bytes=64000 * 1024
        ),
    )(
        bound_now[:, :, 0], bound_new[:, 0], value_weight[0], out_weight[0],
        inputs_saved[:, :, 0], queries_saved[:, :, 0], keys_saved[:, :, 0], grad_now[:, 0], grad_new,
    )
    mean_out = gsum[:TOK]
    tail = gsum[TOK:]
    mean_value = jnp.concatenate([tail[:, j * KVW : (j + 1) * KVW] for j in range(4)], axis=0)
    value_moment_new = decay_rate * value_moment + mean_value[None]
    out_moment_new = decay_rate * out_moment + mean_out[None]
    value_weight_new = value_weight - learn_rate * value_moment_new
    out_weight_new = out_weight - learn_rate * out_moment_new
    return (
        gi[:, :, None], dq[:, :, None], dk[:, :, None],
        value_weight_new, out_weight_new, value_moment_new, out_moment_new,
    )


def solution(mesh):
    return jax.shard_map(
        shards,
        mesh=mesh,
        in_specs=(
            P("section", "lane", None),
            P("section", "lane", None),
            P("section", "lane", None),
            P("section", "lane", None),
            P(None, None, "section", "lane", None),
            P(None, None, "section", "lane", None),
            P(None, None, "section", "lane", None),
            P(None, "section", "lane", None),
            P(None, "lane", None),
            P(None, None, "lane"),
            P(None, "lane"),
        ),
        out_specs=(
            P(None, None, "section", "lane", None),
            P(None, None, "section", "lane", None),
            P(None, None, "section", "lane", None),
            P("section", "lane", None),
            P("section", "lane", None),
            P("section", "lane", None),
            P("section", "lane", None),
        ),
        check_vma=False,
    )
```

```python
import functools
import math

import jax
import jax.numpy as jnp
from jax import lax
from jax.experimental import pallas as pl
from jax.experimental.pallas import tpu as pltpu
from jax.sharding import PartitionSpec as P

TOK = 128
D = 1024
QW = 2048
KVW = 256
HS = 128
HEADS = 16
GROUP = 8
LANES = 16
ROWS = 144
CUT = 80
VROWS = 16
HALF = TOK // 2
WIDE = D // 2

decay_rate = 0.9
learn_rate = 0.01
MESH = pl.DeviceIdType.MESH
bf16 = jnp.bfloat16
f32 = jnp.float32

PLACES = ((2, 1), (1, 1), (3, 1), (2, 0), (1, 0), (3, 0), (0, 1), (0, 0))


def dot(a, b, dims):
    return lax.dot_general(a, b, (dims, ((), ())), preferred_element_type=f32)


def kernel(
    sections,
    bn, bw, wv_in, wo_in, x_hbm, q_hbm, k_hbm, gnow_hbm, gnew_hbm,
    gi_hbm, dq_hbm, dk_hbm, fo_hbm, fv_hbm, mo_hbm, mv_hbm,
    wb, wvs, xs, qs, ks, gs, gnews, pr, vs, at, ga, dvs, gis, dqs, dks, rx,
    dwv, pc, po, rc, rn, pcv, pov, rcv, rnv, msend, msendv, fin, finv, maskb,
    ld_sem, st_sem, ag_send, ag_recv, rs_send, rs_recv, rv_send, rv_recv, ms_send, ms_recv, nb_send, nb_recv,
):
    s = lax.axis_index("section")
    l = lax.axis_index("lane")
    y = l // 4
    x = (l // 2) % 2
    c = l % 2
    scale = 1.0 / math.sqrt(HS)

    def lane(dy, dx, dc):
        yy = (y + dy) % 4
        xx = (x + dx) % 2
        cc = (c + dc) % 2
        return yy * 4 + xx * 2 + cc

    def slot(q, dy, dx, dc):
        return lane(dy, dx + q, dc)

    xp = (s, lane(0, 1, 0))
    yp = (s, lane(1, 0, 0))
    ym = (s, lane(3, 0, 0))
    cp = (s, lane(0, 0, 1))
    mir = (sections - 1 - s, lane(0, 1, 0))
    before = ((s + sections - 1) % sections, l)
    after = ((s + 1) % sections, l)

    loads = [
        pltpu.make_async_copy(k_hbm, ks, ld_sem.at[0]),
        pltpu.make_async_copy(q_hbm, qs, ld_sem.at[1]),
        pltpu.make_async_copy(x_hbm, xs, ld_sem.at[2]),
        pltpu.make_async_copy(gnow_hbm, gs.at[:, 0], ld_sem.at[3]),
        pltpu.make_async_copy(gnew_hbm, gnews, ld_sem.at[4]),
    ]
    for cpy in loads:
        cpy.start()

    barrier = pltpu.get_barrier_semaphore()
    peers = (xp, yp, ym, cp, mir, before, after) + tuple((s, lane(dy, dx, 0)) for dy, dx in PLACES[:4])
    for p in peers:
        pl.semaphore_signal(barrier, inc=1, device_id=p, device_id_type=MESH)
    wb[0, l, :TOK, :] = wo_in[...].astype(bf16)
    for j in range(4):
        wb[0, l, TOK:, j * KVW : (j + 1) * KVW] = wv_in[16 * j : 16 * (j + 1), :].astype(bf16)
    pl.semaphore_wait(barrier, len(peers))

    sent = []

    def send(src, dst, ssem, rsem, dev):
        cpy = pltpu.make_async_remote_copy(
            src_ref=src, dst_ref=dst, send_sem=ssem, recv_sem=rsem, device_id=dev, device_id_type=MESH
        )
        cpy.start()
        sent.append(cpy)

    def arrived(dst, sem):
        pltpu.make_async_copy(dst, dst, sem).wait()

    OWN, X, A, B, OPP, AX, BX, OX = range(8)
    where_is = {
        OWN: (0, 0), X: (0, 1), A: (3, 0), B: (1, 0), OPP: (2, 0), AX: (3, 1), BX: (1, 1), OX: (2, 1),
    }

    def block(q, kind, core=0):
        return wb.at[q, slot(q, *where_is[kind], core)]

    def ag_send_block(q, n, kind, to, rkind, rows=None):
        ref = block(q, kind)
        if rows is not None:
            ref = ref.at[pl.ds(*rows), :]
        send(ref, ref, ag_send.at[q, n], ag_recv.at[q, rkind], to)

    def ag_core(q, kind):
        ref = block(q, kind)
        send(ref, ref, ag_send.at[q, 8 + kind], ag_recv.at[q, 8 + kind], cp)

    def ag_start(q):
        ag_send_block(q, 0, OWN, yp, 1, (0, CUT))
        ag_send_block(q, 1, OWN, ym, 2, (CUT, ROWS - CUT))
        ag_send_block(q, 2, OWN, xp, 0)
        ag_send_block(q, 16, OWN, yp, 16, (CUT, ROWS - CUT))
        ag_send_block(q, 17, OWN, ym, 17, (0, CUT))
        ag_core(q, OWN)

    def part(q, kind, first):
        return block(q, kind).at[pl.ds(*((0, CUT) if first else (CUT, ROWS - CUT))), :]

    def ag_step1(q):
        arrived(part(q, A, True), ag_recv.at[q, 1])
        ag_send_block(q, 3, A, yp, 3, (0, CUT))
        arrived(part(q, B, False), ag_recv.at[q, 2])
        ag_send_block(q, 4, B, ym, 4, (CUT, ROWS - CUT))

    def ag_step1b(q):
        arrived(block(q, X), ag_recv.at[q, 0])
        ag_send_block(q, 5, X, yp, 5)
        ag_send_block(q, 6, X, ym, 6)
        arrived(part(q, A, False), ag_recv.at[q, 16])
        ag_core(q, A)
        arrived(part(q, B, True), ag_recv.at[q, 17])
        ag_core(q, B)
        ag_core(q, X)

    def ag_step2(q):
        arrived(part(q, OPP, True), ag_recv.at[q, 3])
        arrived(part(q, OPP, False), ag_recv.at[q, 4])
        ag_send_block(q, 7, OPP, xp, 7)
        ag_core(q, OPP)

    def ag_step3(q):
        arrived(block(q, AX), ag_recv.at[q, 5])
        ag_core(q, AX)
        arrived(block(q, BX), ag_recv.at[q, 6])
        ag_core(q, BX)
        arrived(block(q, OX), ag_recv.at[q, 7])
        ag_core(q, OX)

    def grad_attended(q, kinds):
        for kind in kinds:
            arrived(block(q, kind, 1), ag_recv.at[q, 8 + kind])
            n = slot(q, *where_is[kind], 0) // 2
            w2 = jnp.concatenate([wb[q, 2 * n, :TOK, :], wb[q, 2 * n + 1, :TOK, :]], axis=0)
            r = dot(gs[q, 0], w2, ((1,), (1,))).astype(bf16)
            ga[q, 0, 2 * n] = r[:, :HS]
            ga[q, 0, 2 * n + 1] = r[:, HS:]

    def value_rows(q):
        @pl.loop(0, LANES)
        def _(h):
            for j in range(4):
                at_row = pl.multiple_of(h * 64 + 16 * j, 16)
                wvs[q, pl.ds(at_row, 16), :] = wb[q, h, TOK:, j * KVW : (j + 1) * KVW]

    stores = []

    def store(src, dst):
        cpy = pltpu.make_async_copy(src, dst, st_sem.at[len(stores)])
        cpy.start()
        stores.append(cpy)

    def softmax(q, t):
        here = bn[q, s]
        if t == 0:
            bound = here
        elif q == 0:
            bound = jnp.where(s == sections - 1, bw[0], bn[0, jnp.minimum(s + 1, sections - 1)])
        else:
            bound = jnp.where(s == 0, bw[1], bn[1, jnp.maximum(s - 1, 0)])
        row = lax.broadcasted_iota(jnp.int32, (TOK, TOK), 0)
        col = lax.broadcasted_iota(jnp.int32, (TOK, TOK), 1)
        seen = (col <= row) & ((col >= bound) | (row < bound))
        maskb[...] = jnp.where(seen, 0.0, -1e30).astype(f32)
        for g in range(2):
            kg = ks[q, t, :, g * HS : (g + 1) * HS]

            @pl.loop(0, GROUP // 2)
            def _(n):
                for u in range(2):
                    h = g * GROUP + n * 2 + u
                    qh = qs[q, t, :, pl.ds(pl.multiple_of(h * HS, HS), HS)]
                    sc = dot(qh, kg, ((1,), (1,))) * scale + maskb[...]
                    e = jnp.exp(sc - jnp.max(sc, axis=-1, keepdims=True))
                    pr[q, t, h] = e * (1.0 / jnp.sum(e, axis=-1, keepdims=True))

    def values(q):
        for t in range(2):
            vs[q, t] = dot(xs[q, t], wvs[q], ((1,), (0,))).astype(bf16)

    def attended(q, t):
        for g in range(2):
            vg = vs[q, t, :, g * HS : (g + 1) * HS]

            @pl.loop(0, GROUP // 2)
            def _(n):
                for u in range(2):
                    h = g * GROUP + n * 2 + u
                    at[q, h, t * TOK : (t + 1) * TOK, :] = dot(pr[q, t, h].astype(bf16), vg, ((1,), (0,))).astype(bf16)

    def grad_attended_late(q):
        @pl.loop(0, HEADS // 2)
        def _(n):
            w2 = jnp.concatenate([wb[q, 2 * n, :TOK, :], wb[q, 2 * n + 1, :TOK, :]], axis=0)
            r = dot(gs[q, 1], w2, ((1,), (1,))).astype(bf16)
            ga[q, 1, 2 * n] = r[:, :HS]
            ga[q, 1, 2 * n + 1] = r[:, HS:]

    def grad_values(q, t):
        for g in range(2):
            p8 = pr[q, t, g * GROUP : (g + 1) * GROUP].astype(bf16).reshape(GROUP * TOK, TOK)
            g8 = ga[q, t, g * GROUP : (g + 1) * GROUP].reshape(GROUP * TOK, HS)
            dvs[q, t, :, g * HS : (g + 1) * HS] = dot(p8, g8, ((0,), (0,))).astype(bf16)
        for n in range(4):
            cols = slice(n * 256, (n + 1) * 256)
            add = dot(dvs[q, t], wvs[q, cols, :], ((1,), (1,)))
            gis[q, t, :, cols] = (gs[q, t, :, cols].astype(f32) + add).astype(bf16)
            if t == 0 and n % 2:
                send(
                    gis.at[q, 0, :, pl.ds(n // 2 * WIDE, WIDE)], rx.at[q, n // 2],
                    nb_send.at[q, n // 2], nb_recv.at[q, n // 2], before if q == 0 else after,
                )
        store(gis.at[q, t], gi_hbm.at[q, t])

    def take(q, n):
        arrived(rx.at[q, n], nb_recv.at[q, n])
        at_end = s == (sections - 1 if q == 0 else 0)
        cols = slice(n * WIDE, (n + 1) * WIDE)
        gs[q, 1, :, cols] = jnp.where(at_end, gnews[q, :, cols], rx[q, n])

    def score_grads(q, t, only=None):
        for g in range(2) if only is None else (only,):
            kg = ks[q, t, :, g * HS : (g + 1) * HS]
            vg = vs[q, t, :, g * HS : (g + 1) * HS]

            def body(n, acc):
                for u in range(2):
                    h = g * GROUP + n * 2 + u
                    at_col = pl.ds(pl.multiple_of(h * HS, HS), HS)
                    gp = dot(ga[q, t, h], vg, ((1,), (1,)))
                    p = pr[q, t, h]
                    delta = jnp.sum(p * gp, axis=-1, keepdims=True)
                    ds = (p * (gp - delta) * scale).astype(bf16)
                    dqs[q, t, :, at_col] = dot(ds, kg, ((1,), (0,))).astype(bf16)
                    acc = acc + dot(ds, qs[q, t, :, at_col], ((0,), (0,)))
                return acc

            acc = lax.fori_loop(0, GROUP // 2, body, jnp.zeros((TOK, HS), f32))
            dks[q, t, :, g * HS : (g + 1) * HS] = acc.astype(bf16)

    def store_scores(q, t):
        store(dqs.at[q, t], dq_hbm.at[q, t])
        store(dks.at[q, t], dk_hbm.at[q, t])

    def rs_blocks(q, k, places=(0, 1, 2, 3, 4, 5, 6, 7)):
        def one(ref, i, dc):
            r = slot(q, *PLACES[i], dc)
            a = at[q, r]
            gg = gs[q, :, :, k * WIDE : (k + 1) * WIDE].reshape(2 * TOK, WIDE)
            ref[q, k, i] = dot(a, gg, ((0,), (0,))).astype(bf16)

        for i in places:
            one(pc, i, 1)
            send(pc.at[q, k, i], rc.at[q, k, i], rs_send.at[q, k, 11 + i], rs_recv.at[q, k, 11 + i], cp)
        for i in places:
            one(po, i, 0)

    R1A, R1B, R2A, R2B, R3A, R3B, R4AE, R4AL, R4BE, R4BL, R5 = range(11)
    UP, LOW, ALL = (0, HALF), (HALF, HALF), (0, TOK)
    PLACE_OF = {R1A: 0, R1B: 0, R2A: 1, R2B: 2, R3A: 3, R3B: 3, R4AE: 4, R4AL: 4, R4BE: 5, R4BL: 5, R5: 6}

    def rows_of(ref, rows):
        return ref.at[pl.ds(*rows), :]

    def rs_core(q, k, i):
        arrived(rc.at[q, k, i], rs_recv.at[q, k, 11 + i])

    def rs_hop(q, k, n, i, to, rows=ALL):
        send(
            rows_of(po.at[q, k, i], rows), rows_of(rn.at[q, k, PLACE_OF[n]], rows),
            rs_send.at[q, k, n], rs_recv.at[q, k, n], to,
        )

    def rs_got(q, k, n, rows=ALL):
        arrived(rows_of(rn.at[q, k, PLACE_OF[n]], rows), rs_recv.at[q, k, n])

    def add_in(q, k, i, more, rows=ALL, core=True):
        rr = slice(rows[0], rows[0] + rows[1])
        total = po[q, k, i, rr, :].astype(f32)
        if core:
            total = total + rc[q, k, i, rr, :].astype(f32)
        for n in more:
            total = total + rn[q, k, PLACE_OF[n], rr, :].astype(f32)
        return total

    def put(q, k, i, more, rows=ALL, core=True):
        po[q, k, i, rows[0] : rows[0] + rows[1], :] = add_in(q, k, i, more, rows, core).astype(bf16)

    def rs_a(q, k):
        rs_core(q, k, 0)
        put(q, k, 0, ())
        rs_hop(q, k, R1A, 0, xp, UP)
        rs_hop(q, k, R1B, 0, xp, LOW)
        rs_core(q, k, 1)
        put(q, k, 1, ())
        rs_hop(q, k, R2A, 1, yp)
        rs_core(q, k, 2)
        put(q, k, 2, ())
        rs_hop(q, k, R2B, 2, ym)

    def rs_early(q, k):
        rs_core(q, k, 4)
        put(q, k, 4, ())
        rs_hop(q, k, R4AE, 4, yp, LOW)
        rs_core(q, k, 5)
        put(q, k, 5, ())
        rs_hop(q, k, R4BE, 5, ym, UP)

    def rs_b(q, k):
        rs_core(q, k, 3)
        rs_got(q, k, R1A, UP)
        put(q, k, 3, (R1A,), UP)
        rs_hop(q, k, R3A, 3, yp, UP)
        rs_got(q, k, R1B, LOW)
        put(q, k, 3, (R1B,), LOW)
        rs_hop(q, k, R3B, 3, ym, LOW)

    def rs_b2(q, k):
        rs_core(q, k, 6)
        rs_got(q, k, R2A)
        rs_got(q, k, R2B)
        put(q, k, 6, (R2A, R2B))
        rs_hop(q, k, R5, 6, xp)

    def rs_c(q, k):
        rs_got(q, k, R3A, UP)
        put(q, k, 4, (R3A,), UP, False)
        rs_hop(q, k, R4AL, 4, yp, UP)
        rs_got(q, k, R3B, LOW)
        put(q, k, 5, (R3B,), LOW, False)
        rs_hop(q, k, R4BL, 5, ym, LOW)

    VC = 7

    def rv_start(q):
        xt = xs[q].reshape(2 * TOK, D)
        dv = dvs[q].reshape(2 * TOK, KVW)
        for n in range(4):
            dwv[q, n * 256 : (n + 1) * 256, :] = dot(xt[:, n * 256 : (n + 1) * 256], dv, ((0,), (0,))).astype(bf16)
        for ref, dc in ((pcv, 1), (pov, 0)):
            for i in range(8):
                r = slot(q, *PLACES[i], dc)
                for j in range(4):
                    at_row = pl.multiple_of(r * 64 + 16 * j, 16)
                    ref[q, i, :, j * KVW : (j + 1) * KVW] = dwv[q, pl.ds(at_row, 16), :]
            if dc == 1:
                send(pcv.at[q], rcv.at[q], rv_send.at[q, VC], rv_recv.at[q, VC], cp)

    def rv_a(q):
        arrived(rcv.at[q], rv_recv.at[q, VC])
        for i in range(8):
            pov[q, i] = (pov[q, i].astype(f32) + rcv[q, i].astype(f32)).astype(bf16)
        for i in range(7):
            send(pov.at[q, i], rnv.at[q, i], rv_send.at[q, i], rv_recv.at[q, i], (s, lane(*PLACES[i], 0)))

    def rv_final(q):
        total = pov[q, 7].astype(f32)
        for i in range(7):
            arrived(rnv.at[q, i], rv_recv.at[q, i])
            total = total + rnv[q, i].astype(f32)
        if q == 0:
            finv[...] = total
            store(finv, fv_hbm)
        else:
            msendv[...] = total.astype(bf16)
            send(msendv, mv_hbm, ms_send.at[3], ms_recv.at[3], mir)

    def rs_final(q, k):
        rs_core(q, k, 7)
        rs_got(q, k, R5)
        rs_got(q, k, R4AE, LOW)
        rs_got(q, k, R4BE, UP)
        rs_got(q, k, R4AL, UP)
        rs_got(q, k, R4BL, LOW)
        for rows in (UP, LOW):
            total = add_in(q, k, 7, (R4AL, R4BL, R5), rows)
            here = slice(rows[0], rows[0] + rows[1])
            if q == 0:
                fin[k, here, :] = total
            else:
                msend[k, here, :] = total.astype(bf16)
        if q == 0:
            store(fin.at[k], fo_hbm.at[k])
        else:
            send(msend.at[k], mo_hbm.at[k], ms_send.at[1 + k], ms_recv.at[1 + k], mir)

    own = block(0, OWN)
    send(own, wb.at[1, l], ms_send.at[0], ms_recv.at[0], mir)
    ag_start(0)
    loads[0].wait()
    loads[1].wait()
    softmax(0, 0)
    ag_step1(0)
    softmax(0, 1)
    ag_step1b(0)
    softmax(1, 0)
    ag_step2(0)
    loads[2].wait()
    loads[3].wait()
    loads[4].wait()
    grad_attended(0, (OWN, A, B, X))
    arrived(block(1, OWN), ms_recv.at[0])
    ag_start(1)
    softmax(1, 1)
    ag_step3(0)
    grad_attended(0, (OPP,))
    ag_step1(1)
    grad_attended(0, (AX, BX, OX))
    value_rows(0)
    grad_values(0, 0)
    values(0)
    attended(0, 0)
    ag_step1b(1)
    attended(0, 1)
    ag_step2(1)
    take(0, 0)
    rs_blocks(0, 0)
    rs_a(0, 0)
    take(0, 1)
    rs_blocks(0, 1)
    rs_a(0, 1)
    grad_attended(1, (OWN, A, B, X))
    ag_step3(1)
    score_grads(0, 0, 0)
    rs_b(0, 0)
    rs_early(0, 0)
    grad_attended(1, (OPP, AX, BX, OX))
    value_rows(1)
    grad_values(1, 0)
    rs_b2(0, 0)
    rs_b(0, 1)
    rs_c(0, 0)
    values(1)
    attended(1, 0)
    rs_b2(0, 1)
    rs_early(0, 1)
    attended(1, 1)
    take(1, 0)
    rs_blocks(1, 0)
    rs_a(1, 0)
    take(1, 1)
    rs_blocks(1, 1)
    rs_a(1, 1)
    grad_attended_late(0)
    rs_b(1, 0)
    rs_early(1, 0)
    grad_values(0, 1)
    rv_start(0)
    rs_b2(1, 0)
    grad_attended_late(1)
    rs_b(1, 1)
    grad_values(1, 1)
    rv_start(1)
    rs_early(1, 1)
    rs_b2(1, 1)
    rv_a(0)
    rs_c(1, 0)
    rv_a(1)
    score_grads(0, 0, 1)
    store_scores(0, 0)
    rs_final(1, 0)
    rs_c(1, 1)
    rs_c(0, 1)
    score_grads(1, 0)
    store_scores(1, 0)
    rs_final(1, 1)
    rv_final(1)
    rs_final(0, 0)
    score_grads(1, 1)
    store_scores(1, 1)
    rs_final(0, 1)
    rv_final(0)
    score_grads(0, 1)
    store_scores(0, 1)
    def ending():
        for n in range(2):
            arrived(mo_hbm.at[n], ms_recv.at[1 + n])
        arrived(mv_hbm, ms_recv.at[3])

    def settle():
        for cpy in stores:
            cpy.wait()

    def leave():
        for cpy in sent:
            cpy.wait_send()

    ending()
    settle()
    leave()


def finish(
    wv_in, wo_in, mv_in, mo_in, fo_in, fv_in, ro_in, rv_in, gi_in, dq_in, dk_in,
    gi, dq, dk, wv_new, wo_new, mv_new, mo_new,
    wv, wo, mv, mo, fo, fv, ro, rv, gib, dqb, dkb, wvb, wob, mvb, mob, in_sem, out_sem,
):
    firsts = [(fo_in, fo), (ro_in, ro), (wo_in, wo), (mo_in, mo), (fv_in, fv), (rv_in, rv), (wv_in, wv), (mv_in, mv)]
    pieces = [(dq_in.at[q, t], dqb.at[q, t], dq.at[q, t]) for q in range(2) for t in range(2)]
    pieces += [(gi_in.at[q], gib.at[q], gi.at[q]) for q in range(2)]
    pieces += [(dk_in, dkb, dk)]
    loads = [pltpu.make_async_copy(a, b, in_sem.at[n]) for n, (a, b, *_) in enumerate(firsts + pieces)]
    for cpy in loads:
        cpy.start()
    stores = []

    def store(src, dst):
        cpy = pltpu.make_async_copy(src, dst, out_sem.at[len(stores)])
        cpy.start()
        stores.append(cpy)

    for cpy in loads[:8]:
        cpy.wait()

    def update(total, w, m, w_buf, m_buf, at):
        moment = decay_rate * m[at] + total / LANES
        m_buf[at] = moment
        w_buf[at] = w[at] - learn_rate * moment

    for n in range(2):
        update(fo[n] + ro[n].astype(f32), wo, mo, wob, mob, (slice(None), slice(n * WIDE, (n + 1) * WIDE)))
    store(mob, mo_new)
    store(wob, wo_new)
    total = fv[...] + rv[...].astype(f32)
    for j in range(4):
        update(total[:, j * KVW : (j + 1) * KVW], wv, mv, wvb, mvb, (slice(16 * j, 16 * (j + 1)), slice(None)))
    store(mvb, mv_new)
    store(wvb, wv_new)
    for cpy, (_, b, c) in zip(loads[8:], pieces):
        cpy.wait()
        store(b, c)
    for cpy in stores:
        cpy.wait()


def shards(
    value_weight, out_weight, value_moment, out_moment, inputs_saved, queries_saved, keys_saved,
    grad_now, grad_new, bound_now, bound_new,
):
    sections = lax.axis_size("section")
    hbm = pl.BlockSpec(memory_space=pltpu.MemorySpace.HBM)
    vmem = pl.BlockSpec(memory_space=pltpu.VMEM)
    smem = pl.BlockSpec(memory_space=pltpu.SMEM)
    dma = pltpu.SemaphoreType.DMA
    gi, dq, dk, fo, fv, ro, rv = pl.pallas_call(
        functools.partial(kernel, sections),
        out_shape=(
            jax.ShapeDtypeStruct((2, 2, TOK, D), bf16),
            jax.ShapeDtypeStruct((2, 2, TOK, QW), bf16),
            jax.ShapeDtypeStruct((2, 2, TOK, KVW), bf16),
            jax.ShapeDtypeStruct((2, TOK, WIDE), f32),
            jax.ShapeDtypeStruct((VROWS, D), f32),
            jax.ShapeDtypeStruct((2, TOK, WIDE), bf16),
            jax.ShapeDtypeStruct((VROWS, D), bf16),
        ),
        in_specs=[smem, smem, vmem, vmem, hbm, hbm, hbm, hbm, hbm],
        out_specs=(hbm,) * 7,
        scratch_shapes=[
            pltpu.VMEM((2, LANES, ROWS, D), bf16),
            pltpu.VMEM((2, D, KVW), bf16),
            pltpu.VMEM((2, 2, TOK, D), bf16),
            pltpu.VMEM((2, 2, TOK, QW), bf16),
            pltpu.VMEM((2, 2, TOK, KVW), bf16),
            pltpu.VMEM((2, 2, TOK, D), bf16),
            pltpu.VMEM((2, TOK, D), bf16),
            pltpu.VMEM((2, 2, HEADS, TOK, TOK), f32),
            pltpu.VMEM((2, 2, TOK, KVW), bf16),
            pltpu.VMEM((2, HEADS, 2 * TOK, HS), bf16),
            pltpu.VMEM((2, 2, HEADS, TOK, HS), bf16),
            pltpu.VMEM((2, 2, TOK, KVW), bf16),
            pltpu.VMEM((2, 2, TOK, D), bf16),
            pltpu.VMEM((2, 2, TOK, QW), bf16),
            pltpu.VMEM((2, 2, TOK, KVW), bf16),
            pltpu.VMEM((2, 2, TOK, WIDE), bf16),
            pltpu.VMEM((2, D, KVW), bf16),
            pltpu.VMEM((2, 2, 8, TOK, WIDE), bf16),
            pltpu.VMEM((2, 2, 8, TOK, WIDE), bf16),
            pltpu.VMEM((2, 2, 8, TOK, WIDE), bf16),
            pltpu.VMEM((2, 2, 7, TOK, WIDE), bf16),
            pltpu.VMEM((2, 8, VROWS, D), bf16),
            pltpu.VMEM((2, 8, VROWS, D), bf16),
            pltpu.VMEM((2, 8, VROWS, D), bf16),
            pltpu.VMEM((2, 7, VROWS, D), bf16),
            pltpu.VMEM((2, TOK, WIDE), bf16),
            pltpu.VMEM((VROWS, D), bf16),
            pltpu.VMEM((2, TOK, WIDE), f32),
            pltpu.VMEM((VROWS, D), f32),
            pltpu.VMEM((TOK, TOK), f32),
            dma((5,)),
            dma((15,)),
            dma((2, 18)),
            dma((2, 18)),
            dma((2, 2, 19)),
            dma((2, 2, 19)),
            dma((2, 8)),
            dma((2, 8)),
            dma((4,)),
            dma((4,)),
            dma((2, 2)),
            dma((2, 2)),
        ],
        compiler_params=pltpu.CompilerParams(
            collective_id=0, has_side_effects=True, vmem_limit_bytes=64000 * 1024
        ),
    )(
        bound_now[:, :, 0], bound_new[:, 0], value_weight[0], out_weight[0],
        inputs_saved[:, :, 0], queries_saved[:, :, 0], keys_saved[:, :, 0], grad_now[:, 0], grad_new,
    )
    big = jax.ShapeDtypeStruct((TOK, D), f32)
    small = jax.ShapeDtypeStruct((64, KVW), f32)
    gi, dq, dk, wv, wo, mv, mo = pl.pallas_call(
        finish,
        out_shape=(
            jax.ShapeDtypeStruct((2, 2, TOK, D), bf16),
            jax.ShapeDtypeStruct((2, 2, TOK, QW), bf16),
            jax.ShapeDtypeStruct((2, 2, TOK, KVW), bf16),
            small, big, small, big,
        ),
        in_specs=[hbm] * 11,
        out_specs=(hbm,) * 7,
        scratch_shapes=[
            pltpu.VMEM((64, KVW), f32),
            pltpu.VMEM((TOK, D), f32),
            pltpu.VMEM((64, KVW), f32),
            pltpu.VMEM((TOK, D), f32),
            pltpu.VMEM((2, TOK, WIDE), f32),
            pltpu.VMEM((VROWS, D), f32),
            pltpu.VMEM((2, TOK, WIDE), bf16),
            pltpu.VMEM((VROWS, D), bf16),
            pltpu.VMEM((2, 2, TOK, D), bf16),
            pltpu.VMEM((2, 2, TOK, QW), bf16),
            pltpu.VMEM((2, 2, TOK, KVW), bf16),
            pltpu.VMEM((64, KVW), f32),
            pltpu.VMEM((TOK, D), f32),
            pltpu.VMEM((64, KVW), f32),
            pltpu.VMEM((TOK, D), f32),
            dma((15,)),
            dma((11,)),
        ],
        compiler_params=pltpu.CompilerParams(vmem_limit_bytes=64000 * 1024),
    )(value_weight[0], out_weight[0], value_moment[0], out_moment[0], fo, fv, ro, rv, gi, dq, dk)
    return (gi[:, :, None], dq[:, :, None], dk[:, :, None], wv[None], wo[None], mv[None], mo[None])


def solution(mesh):
    return jax.shard_map(
        shards,
        mesh=mesh,
        in_specs=(
            P("section", "lane", None),
            P("section", "lane", None),
            P("section", "lane", None),
            P("section", "lane", None),
            P(None, None, "section", "lane", None),
            P(None, None, "section", "lane", None),
            P(None, None, "section", "lane", None),
            P(None, "section", "lane", None),
            P(None, "lane", None),
            P(None, None, "lane"),
            P(None, "lane"),
        ),
        out_specs=(
            P(None, None, "section", "lane", None),
            P(None, None, "section", "lane", None),
            P(None, None, "section", "lane", None),
            P("section", "lane", None),
            P("section", "lane", None),
            P("section", "lane", None),
            P("section", "lane", None),
        ),
        check_vma=False,
    )
```

```python
import functools
import math

import jax
import jax.numpy as jnp
from jax import lax
from jax.experimental import pallas as pl
from jax.experimental.pallas import tpu as pltpu
from jax.sharding import PartitionSpec as P

TOK = 128
D = 1024
QW = 2048
KVW = 256
HS = 128
HEADS = 16
GROUP = 8
LANES = 16
ROWS = 144
CUT = 80
VROWS = 16
SIDE = 16
UNROLL = 8
HALF = TOK // 2
WIDE = D // 2

decay_rate = 0.9
learn_rate = 0.01
MESH = pl.DeviceIdType.MESH
bf16 = jnp.bfloat16
f32 = jnp.float32

VPLACES = ((2, 1), (1, 1), (3, 1), (0, 1), (2, 0), (1, 0), (3, 0), (0, 0))
PLACES = ((2, 1), (1, 1), (3, 1), (2, 0), (1, 0), (3, 0), (0, 1), (0, 0))


def dot(a, b, dims):
    return lax.dot_general(a, b, (dims, ((), ())), preferred_element_type=f32)


def kernel(
    sections,
    bn_in, bw_in, wv_hbm, wo_hbm, x_hbm, q_hbm, k_hbm, gnow_hbm, gnew_hbm,
    gi_hbm, dq_hbm, dk_hbm, fo_hbm, fv_hbm, mo_hbm, mv_hbm,
    wb, wvs, xs, qs, ks, gs, gnews, pr, vs, at, ga, dvs, gis, dqs, dks, rx,
    bn, bw, wv_in, wo_in, dwv, pc, po, rcn, pcv, pov, rvn, msend, msendv, fin, finv, maskb,
    ld_sem, st_sem, ag_done, ag_recv, rs_done, rs_recv, rv_done, rv_recv, ms_send, ms_recv, nb_done, nb_recv,
):
    s = lax.axis_index("section")
    l = lax.axis_index("lane")
    y = l // 4
    x = (l // 2) % 2
    c = l % 2
    scale = 1.0 / math.sqrt(HS)

    def lane(dy, dx, dc):
        yy = (y + dy) % 4
        xx = (x + dx) % 2
        cc = (c + dc) % 2
        return yy * 4 + xx * 2 + cc

    def slot(q, dy, dx, dc):
        return lane(dy, dx + q, dc)

    xp = (s, lane(0, 1, 0))
    yp = (s, lane(1, 0, 0))
    ym = (s, lane(3, 0, 0))
    cp = (s, lane(0, 0, 1))
    y2 = (s, lane(2, 0, 0))
    mir = (sections - 1 - s, lane(0, 1, 0))
    before = ((s + sections - 1) % sections, l)
    after = ((s + 1) % sections, l)

    barrier = pltpu.get_barrier_semaphore()
    peers = (xp, yp, ym, cp, mir, before, after) + (y2,)
    for p in peers:
        pl.semaphore_signal(barrier, inc=1, device_id=p, device_id_type=MESH)
    loads = [
        pltpu.make_async_copy(wo_hbm, wo_in, ld_sem.at[5]),
        pltpu.make_async_copy(wv_hbm, wv_in, ld_sem.at[6]),
        pltpu.make_async_copy(bn_in, bn, ld_sem.at[7]),
        pltpu.make_async_copy(bw_in, bw, ld_sem.at[8]),
        pltpu.make_async_copy(k_hbm, ks, ld_sem.at[0]),
        pltpu.make_async_copy(q_hbm, qs, ld_sem.at[1]),
        pltpu.make_async_copy(x_hbm, xs, ld_sem.at[2]),
        pltpu.make_async_copy(gnow_hbm, gs.at[:, 0], ld_sem.at[3]),
        pltpu.make_async_copy(gnew_hbm, gnews, ld_sem.at[4]),
    ]
    for cpy in loads:
        cpy.start()
    loads[0].wait()
    loads[1].wait()
    wb[0, l, :TOK, :] = wo_in[...].astype(bf16)
    for j in range(4):
        wb[0, l, TOK:, j * KVW : (j + 1) * KVW] = wv_in[16 * j : 16 * (j + 1), :].astype(bf16)
    pl.semaphore_wait(barrier, len(peers))

    def send(src, dst, ssem, rsem, dev):
        cpy = pltpu.make_async_remote_copy(
            src_ref=src, dst_ref=dst, send_sem=ssem, recv_sem=rsem, device_id=dev, device_id_type=MESH
        )
        cpy.start()

    def arrived(dst, sem):
        pltpu.make_async_copy(dst, dst, sem).wait()

    OWN, X, A, B, OPP, AX, BX, OX = range(8)
    where_is = {
        OWN: (0, 0), X: (0, 1), A: (3, 0), B: (1, 0), OPP: (2, 0), AX: (3, 1), BX: (1, 1), OX: (2, 1),
    }

    def block(q, kind, core=0):
        return wb.at[q, slot(q, *where_is[kind], core)]

    def piece(q, kind, n, core=0):
        return block(q, kind, core).at[pl.ds(0, CUT) if n == 0 else pl.ds(CUT, ROWS - CUT), :]

    def most(q, kind):
        return block(q, kind).at[pl.ds(CUT, TOK - CUT), :]

    def rest(q, kind):
        return block(q, kind).at[pl.ds(TOK, VROWS), :]

    def ag_send(q, kind, n, to, as_kind):
        ref = piece(q, kind, n)
        send(ref, ref, ag_done.at[q], ag_recv.at[q, as_kind * 2 + n], to)

    def ag_send_most(q, kind, to, as_kind):
        ref = most(q, kind)
        send(ref, ref, ag_done.at[q], ag_recv.at[q, as_kind * 2 + 1], to)

    def ag_send_rest(q, kind, as_kind):
        ref = rest(q, kind)
        send(ref, ref, ag_done.at[q], ag_recv.at[q, 32 + as_kind - AX], xp)

    def ag_core(q, kind, n):
        ref = piece(q, kind, n)
        send(ref, ref, ag_done.at[q], ag_recv.at[q, 16 + kind * 2 + n], cp)

    def ag_got(q, kind, n, core=0):
        arrived(piece(q, kind, n, core), ag_recv.at[q, core * 16 + kind * 2 + n])

    def ag_start(q):
        ag_send(q, OWN, 0, yp, A)
        ag_send(q, OWN, 1, ym, B)
        ag_send(q, OWN, 0, xp, X)
        ag_send(q, OWN, 1, yp, A)
        ag_send(q, OWN, 0, ym, B)
        ag_send(q, OWN, 1, xp, X)
        ag_core(q, OWN, 0)
        ag_core(q, OWN, 1)

    def ag_step1(q):
        ag_got(q, A, 0)
        ag_send(q, A, 0, yp, OPP)
        ag_got(q, B, 1)
        ag_send(q, B, 1, ym, OPP)
        ag_core(q, A, 0)
        ag_core(q, B, 1)
        ag_got(q, X, 0)
        ag_send(q, X, 0, yp, AX)
        ag_send(q, X, 0, ym, BX)
        ag_core(q, X, 0)

    def ag_step1b(q):
        ag_got(q, X, 1)
        ag_send_most(q, X, yp, AX)
        ag_send_most(q, X, ym, BX)
        ag_core(q, X, 1)
        ag_got(q, A, 1)
        ag_send_rest(q, A, AX)
        ag_send_rest(q, B, BX)
        ag_core(q, A, 1)
        ag_got(q, B, 0)
        ag_core(q, B, 0)

    def ag_step2(q):
        for n in range(2):
            ag_got(q, OPP, n)
            ag_send(q, OPP, n, xp, OX)
            ag_core(q, OPP, n)

    def ag_step3(q, n):
        for kind in (AX, BX):
            if n == 0:
                ag_got(q, kind, 0)
            else:
                arrived(rest(q, kind), ag_recv.at[q, 32 + kind - AX])
                arrived(most(q, kind), ag_recv.at[q, kind * 2 + 1])
            ag_core(q, kind, n)
        ag_got(q, OX, n)
        ag_core(q, OX, n)

    def grad_attended(q, kinds):
        for kind in kinds:
            ag_got(q, kind, 0, 1)
            ag_got(q, kind, 1, 1)
            n = slot(q, *where_is[kind], 0) // 2
            w2 = jnp.concatenate([wb[q, 2 * n, :TOK, :], wb[q, 2 * n + 1, :TOK, :]], axis=0)
            r = dot(gs[q, 0], w2, ((1,), (1,))).astype(bf16)
            ga[q, 0, 2 * n] = r[:, :HS]
            ga[q, 0, 2 * n + 1] = r[:, HS:]

    def value_rows(q):
        @pl.loop(0, LANES)
        def _(h):
            for j in range(4):
                at_row = pl.multiple_of(h * 64 + 16 * j, 16)
                wvs[q, pl.ds(at_row, 16), :] = wb[q, h, TOK:, j * KVW : (j + 1) * KVW]

    stores = []

    def store(src, dst):
        cpy = pltpu.make_async_copy(src, dst, st_sem.at[len(stores)])
        cpy.start()
        stores.append(cpy)

    def softmax(q, t):
        here = bn[q, s]
        if t == 0:
            bound = here
        elif q == 0:
            bound = jnp.where(s == sections - 1, bw[0], bn[0, jnp.minimum(s + 1, sections - 1)])
        else:
            bound = jnp.where(s == 0, bw[1], bn[1, jnp.maximum(s - 1, 0)])
        row = lax.broadcasted_iota(jnp.int32, (TOK, TOK), 0)
        col = lax.broadcasted_iota(jnp.int32, (TOK, TOK), 1)
        seen = (col <= row) & ((col >= bound) | (row < bound))
        maskb[...] = jnp.where(seen, 0.0, -1e30).astype(f32)
        for g in range(2):
            kg = ks[q, t, :, g * HS : (g + 1) * HS]

            @pl.loop(0, GROUP // UNROLL)
            def _(n):
                for u in range(UNROLL):
                    h = g * GROUP + n * UNROLL + u
                    qh = qs[q, t, :, pl.ds(pl.multiple_of(h * HS, HS), HS)]
                    sc = dot(qh, kg, ((1,), (1,))) * scale + maskb[...]
                    e = jnp.exp(sc - jnp.max(sc, axis=-1, keepdims=True))
                    pr[q, t, h] = e * (1.0 / jnp.sum(e, axis=-1, keepdims=True))

    def values(q):
        for t in range(2):
            vs[q, t] = dot(xs[q, t], wvs[q], ((1,), (0,))).astype(bf16)

    def attended(q, t):
        for g in range(2):
            vg = vs[q, t, :, g * HS : (g + 1) * HS]

            @pl.loop(0, GROUP // 4)
            def _(n):
                for u in range(4):
                    h = g * GROUP + n * 4 + u
                    at[q, h, t * TOK : (t + 1) * TOK, :] = dot(pr[q, t, h].astype(bf16), vg, ((1,), (0,))).astype(bf16)

    def grad_attended_late(q, half):
        @pl.loop(half * HEADS // 4, (half + 1) * HEADS // 4)
        def _(n):
            w2 = jnp.concatenate([wb[q, 2 * n, :TOK, :], wb[q, 2 * n + 1, :TOK, :]], axis=0)
            r = dot(gs[q, 1], w2, ((1,), (1,))).astype(bf16)
            ga[q, 1, 2 * n] = r[:, :HS]
            ga[q, 1, 2 * n + 1] = r[:, HS:]

    def grad_values(q, t):
        for g in range(2):
            p8 = pr[q, t, g * GROUP : (g + 1) * GROUP].astype(bf16).reshape(GROUP * TOK, TOK)
            g8 = ga[q, t, g * GROUP : (g + 1) * GROUP].reshape(GROUP * TOK, HS)
            dvs[q, t, :, g * HS : (g + 1) * HS] = dot(p8, g8, ((0,), (0,))).astype(bf16)
        for n in range(4):
            cols = slice(n * 256, (n + 1) * 256)
            add = dot(dvs[q, t], wvs[q, cols, :], ((1,), (1,)))
            gis[q, t, :, cols] = (gs[q, t, :, cols].astype(f32) + add).astype(bf16)
            if t == 0 and n % 2:
                send(
                    gis.at[q, 0, :, pl.ds(n // 2 * WIDE, WIDE)], rx.at[q, n // 2],
                    nb_done.at[q], nb_recv.at[q, n // 2], before if q == 0 else after,
                )
        store(gis.at[q, t], gi_hbm.at[q, t])

    def take(q, n):
        arrived(rx.at[q, n], nb_recv.at[q, n])
        at_end = s == (sections - 1 if q == 0 else 0)
        cols = slice(n * WIDE, (n + 1) * WIDE)
        gs[q, 1, :, cols] = jnp.where(at_end, gnews[q, :, cols], rx[q, n])

    def score_grads(q, t, only=None):
        for g in range(2) if only is None else (only,):
            kg = ks[q, t, :, g * HS : (g + 1) * HS]
            vg = vs[q, t, :, g * HS : (g + 1) * HS]

            def body(n, acc):
                for u in range(UNROLL):
                    h = g * GROUP + n * UNROLL + u
                    at_col = pl.ds(pl.multiple_of(h * HS, HS), HS)
                    gp = dot(ga[q, t, h], vg, ((1,), (1,)))
                    p = pr[q, t, h]
                    delta = jnp.sum(p * gp, axis=-1, keepdims=True)
                    ds = (p * (gp - delta) * scale).astype(bf16)
                    dqs[q, t, :, at_col] = dot(ds, kg, ((1,), (0,))).astype(bf16)
                    acc = acc + dot(ds, qs[q, t, :, at_col], ((0,), (0,)))
                return acc

            acc = lax.fori_loop(0, GROUP // UNROLL, body, jnp.zeros((TOK, HS), f32))
            dks[q, t, :, g * HS : (g + 1) * HS] = acc.astype(bf16)

    def store_scores(q, t):
        store(dqs.at[q, t], dq_hbm.at[q, t])
        store(dks.at[q, t], dk_hbm.at[q, t])

    def rs_blocks(q, k, places=(0, 1, 2, 3, 4, 5, 6, 7)):
        def one(ref, i, dc):
            r = slot(q, *PLACES[i], dc)
            a = at[q, r]
            gg = gs[q, :, :, k * WIDE : (k + 1) * WIDE].reshape(2 * TOK, WIDE)
            ref[q, k, i] = dot(a, gg, ((0,), (0,))).astype(bf16)

        for i in places:
            one(pc, i, 1)
            send(pc.at[q, k, i], rcn.at[q, k, i], rs_done.at[q, k], rs_recv.at[q, k, 11 + i], cp)
        for i in places:
            one(po, i, 0)

    R1A, R1B, R2A, R2B, R3A, R3B, R4AE, R4AL, R4BE, R4BL, R5 = range(11)
    X2A, X2B = 19, 20
    UP, LOW, ALL = (0, HALF), (HALF, HALF), (0, TOK)
    PLACE_OF = {R1A: 0, R1B: 0, R2A: 1, R2B: 2, R3A: 3, R3B: 3, R4AE: 4, R4AL: 4, R4BE: 5, R4BL: 5, R5: 6, X2A: 1, X2B: 2}
    TOP, BOTTOM = (0, SIDE), (TOK - SIDE, SIDE)
    UNDER, ABOVE = (SIDE, TOK - SIDE), (0, TOK - SIDE)

    def rows_of(ref, rows):
        return ref.at[pl.ds(*rows), :]

    def rs_core(q, k, i):
        arrived(rcn.at[q, k, i], rs_recv.at[q, k, 11 + i])

    def rs_hop(q, k, n, i, to, rows=ALL):
        send(
            rows_of(po.at[q, k, i], rows), rows_of(rcn.at[q, k, 8 + PLACE_OF[n]], rows),
            rs_done.at[q, k], rs_recv.at[q, k, n], to,
        )

    def rs_got(q, k, n, rows=ALL):
        arrived(rows_of(rcn.at[q, k, 8 + PLACE_OF[n]], rows), rs_recv.at[q, k, n])

    def add_in(q, k, i, more, rows=ALL):
        rr = slice(rows[0], rows[0] + rows[1])
        total = po[q, k, i, rr, :].astype(f32) + rcn[q, k, i, rr, :].astype(f32)
        for n in more:
            total = total + rcn[q, k, 8 + PLACE_OF[n], rr, :].astype(f32)
        return total

    def put(q, k, i, more, rows=ALL):
        po[q, k, i, rows[0] : rows[0] + rows[1], :] = add_in(q, k, i, more, rows).astype(bf16)

    def rs_a(q, k):
        rs_core(q, k, 0)
        put(q, k, 0, ())
        rs_hop(q, k, R1A, 0, xp, UP)
        rs_hop(q, k, R1B, 0, xp, LOW)
        rs_core(q, k, 1)
        put(q, k, 1, ())
        rs_hop(q, k, R2A, 1, yp, UNDER)
        rs_core(q, k, 2)
        put(q, k, 2, ())
        rs_hop(q, k, R2B, 2, ym, ABOVE)
        rs_hop(q, k, X2A, 1, xp, TOP)
        rs_hop(q, k, X2B, 2, xp, BOTTOM)

    def rs_early(q, k):
        put(q, k, 4, (), LOW)
        rs_hop(q, k, R4AE, 4, yp, LOW)
        put(q, k, 5, (), UP)
        rs_hop(q, k, R4BE, 5, ym, UP)

    def rs_b(q, k):
        for i in (3, 4, 5):
            rs_core(q, k, i)
        rs_got(q, k, R1A, UP)
        put(q, k, 3, (R1A,), UP)
        rs_hop(q, k, R3A, 3, yp, UP)
        rs_got(q, k, R1B, LOW)
        put(q, k, 3, (R1B,), LOW)
        rs_hop(q, k, R3B, 3, ym, LOW)

    def rs_b2(q, k):
        rs_core(q, k, 6)
        rs_got(q, k, R2A, UNDER)
        rs_got(q, k, R2B, ABOVE)
        put(q, k, 6, (R2B,), TOP)
        put(q, k, 6, (R2A, R2B), (SIDE, TOK - 2 * SIDE))
        put(q, k, 6, (R2A,), BOTTOM)
        rs_hop(q, k, R5, 6, xp)

    def rs_c(q, k):
        rs_got(q, k, X2A, TOP)
        rs_got(q, k, R3A, UP)
        put(q, k, 4, (R3A, X2A), TOP)
        put(q, k, 4, (R3A,), (SIDE, HALF - SIDE))
        rs_hop(q, k, R4AL, 4, yp, UP)
        rs_got(q, k, X2B, BOTTOM)
        rs_got(q, k, R3B, LOW)
        put(q, k, 5, (R3B,), (HALF, HALF - SIDE))
        put(q, k, 5, (R3B, X2B), BOTTOM)
        rs_hop(q, k, R4BL, 5, ym, LOW)


    def rv_start(q):
        xt = xs[q].reshape(2 * TOK, D)
        dv = dvs[q].reshape(2 * TOK, KVW)
        for n in range(4):
            dwv[q, n * 256 : (n + 1) * 256, :] = dot(xt[:, n * 256 : (n + 1) * 256], dv, ((0,), (0,))).astype(bf16)
        for ref, dc in ((pcv, 1), (pov, 0)):
            for i in range(8):
                r = slot(q, *VPLACES[i], dc)
                for j in range(4):
                    at_row = pl.multiple_of(r * 64 + 16 * j, 16)
                    ref[q, i, :, j * KVW : (j + 1) * KVW] = dwv[q, pl.ds(at_row, 16), :]
            if dc == 1:
                send(pcv.at[q], rvn.at[q, pl.ds(0, 8)], rv_done.at[q], rv_recv.at[q, 0], cp)

    def rv_a(q):
        arrived(rvn.at[q, pl.ds(0, 8)], rv_recv.at[q, 0])
        for i in range(8):
            pov[q, i] = (pov[q, i].astype(f32) + rvn[q, i].astype(f32)).astype(bf16)
        send(pov.at[q, pl.ds(0, 4)], rvn.at[q, pl.ds(8, 4)], rv_done.at[q], rv_recv.at[q, 1], xp)

    def rv_b(q):
        arrived(rvn.at[q, pl.ds(8, 4)], rv_recv.at[q, 1])
        for i in range(4):
            pov[q, 4 + i] = (pov[q, 4 + i].astype(f32) + rvn[q, 8 + i].astype(f32)).astype(bf16)
        for i, to in ((0, y2), (1, yp), (2, ym)):
            send(pov.at[q, 4 + i], rvn.at[q, 12 + i], rv_done.at[q], rv_recv.at[q, 2 + i], to)

    def rv_final(q):
        total = pov[q, 7].astype(f32)
        for i in range(3):
            arrived(rvn.at[q, 12 + i], rv_recv.at[q, 2 + i])
            total = total + rvn[q, 12 + i].astype(f32)
        if q == 0:
            finv[...] = total
            store(finv, fv_hbm)
        else:
            msendv[...] = total.astype(bf16)
            send(msendv, mv_hbm, ms_send.at[3], ms_recv.at[3], mir)

    def rs_final(q, k):
        rs_core(q, k, 7)
        rs_got(q, k, R5)
        rs_got(q, k, R4AE, LOW)
        rs_got(q, k, R4BE, UP)
        rs_got(q, k, R4AL, UP)
        rs_got(q, k, R4BL, LOW)
        for rows in (UP, LOW):
            total = add_in(q, k, 7, (R4AL, R4BL, R5), rows)
            here = slice(rows[0], rows[0] + rows[1])
            if q == 0:
                fin[k, here, :] = total
            else:
                msend[k, here, :] = total.astype(bf16)
        if q == 0:
            store(fin.at[k], fo_hbm.at[k])
        else:
            send(msend.at[k], mo_hbm.at[k], ms_send.at[1 + k], ms_recv.at[1 + k], mir)

    own = block(0, OWN)
    ag_start(0)
    send(own, wb.at[1, l], ms_send.at[0], ms_recv.at[0], mir)
    for cpy in loads[2:6]:
        cpy.wait()
    softmax(0, 0)
    softmax(0, 1)
    ag_step1(0)
    softmax(1, 0)
    ag_step1b(0)
    softmax(1, 1)
    ag_step2(0)
    for cpy in loads[6:]:
        cpy.wait()
    grad_attended(0, (OWN, A, B, X))
    arrived(block(1, OWN), ms_recv.at[0])
    ag_start(1)
    ag_step3(0, 0)
    grad_attended(0, (OPP,))
    ag_step3(0, 1)
    ag_step1(1)
    grad_attended(0, (AX, BX, OX))
    value_rows(0)
    grad_values(0, 0)
    values(0)
    attended(0, 0)
    ag_step1b(1)
    attended(0, 1)
    ag_step2(1)
    take(0, 0)
    rs_blocks(0, 0)
    rs_a(0, 0)
    grad_attended(1, (OWN, A, B, X))
    ag_step3(1, 0)
    take(0, 1)
    rs_blocks(0, 1)
    ag_step3(1, 1)
    rs_a(0, 1)
    grad_attended(1, (OPP,))
    grad_attended_late(0, 0)
    grad_attended(1, (AX, BX, OX))
    value_rows(1)
    grad_values(1, 0)
    rs_b(0, 0)
    rs_early(0, 0)
    rs_b2(0, 0)
    values(1)
    attended(1, 0)
    rs_b(0, 1)
    attended(1, 1)
    rs_c(0, 0)
    grad_attended_late(0, 1)
    take(1, 0)
    rs_blocks(1, 0)
    rs_a(1, 0)
    take(1, 1)
    rs_blocks(1, 1)
    rs_a(1, 1)
    grad_attended_late(1, 0)
    rs_b(1, 0)
    grad_attended_late(1, 1)
    grad_values(1, 1)
    rv_start(1)
    rs_b2(1, 0)
    rs_b(1, 1)
    rs_early(1, 0)
    rs_c(1, 0)
    rv_a(1)
    rs_b2(1, 1)
    rs_early(1, 1)
    grad_values(0, 1)
    rv_start(0)
    rs_c(1, 1)
    rs_early(0, 1)
    rs_b2(0, 1)
    rv_b(1)
    rs_c(0, 1)
    rv_a(0)
    score_grads(0, 0)
    store_scores(0, 0)
    rs_final(1, 0)
    score_grads(1, 0)
    store_scores(1, 0)
    rs_final(1, 1)
    rv_final(1)
    rv_b(0)
    rs_final(0, 0)
    score_grads(1, 1)
    store_scores(1, 1)
    rs_final(0, 1)
    score_grads(0, 1)
    store_scores(0, 1)
    rv_final(0)
    def ending():
        for n in range(2):
            arrived(mo_hbm.at[n], ms_recv.at[1 + n])
        arrived(mv_hbm, ms_recv.at[3])

    def settle():
        for cpy in stores:
            cpy.wait()

    def leave():
        for q in range(2):
            arrived(wb.at[q, pl.ds(0, 15)], ag_done.at[q])
            for k in range(2):
                arrived(rcn.at[q, k], rs_done.at[q, k])
            arrived(rvn.at[q], rv_done.at[q])
            arrived(rx.at[q], nb_done.at[q])
        arrived(wb.at[1, 0], ms_send.at[0])
        for n in range(2):
            arrived(msend.at[n], ms_send.at[1 + n])
        arrived(msendv, ms_send.at[3])

    ending()
    settle()
    leave()


def finish(
    wv_in, wo_in, mv_in, mo_in, fo_in, fv_in, ro_in, rv_in, gi_in, dq_in, dk_in,
    gi, dq, dk, wv_new, wo_new, mv_new, mo_new,
    wv, wo, mv, mo, fo, fv, ro, rv, gib, dqb, dkb, wvb, wob, mvb, mob, in_sem, out_sem,
):
    firsts = [(fo_in, fo), (ro_in, ro), (wo_in, wo), (mo_in, mo), (fv_in, fv), (rv_in, rv), (wv_in, wv), (mv_in, mv)]
    pieces = [(dq_in.at[q, t], dqb.at[q, t], dq.at[q, t]) for q in range(2) for t in range(2)]
    pieces += [(gi_in.at[q], gib.at[q], gi.at[q]) for q in range(2)]
    pieces += [(dk_in, dkb, dk)]
    loads = [pltpu.make_async_copy(a, b, in_sem.at[n]) for n, (a, b, *_) in enumerate(firsts + pieces)]
    for cpy in loads:
        cpy.start()
    stores = []

    def store(src, dst):
        cpy = pltpu.make_async_copy(src, dst, out_sem.at[len(stores)])
        cpy.start()
        stores.append(cpy)

    for cpy in loads[:8]:
        cpy.wait()

    def update(total, w, m, w_buf, m_buf, at):
        moment = decay_rate * m[at] + total / LANES
        m_buf[at] = moment
        w_buf[at] = w[at] - learn_rate * moment

    for n in range(2):
        update(fo[n] + ro[n].astype(f32), wo, mo, wob, mob, (slice(None), slice(n * WIDE, (n + 1) * WIDE)))
    store(mob, mo_new)
    store(wob, wo_new)
    total = fv[...] + rv[...].astype(f32)
    for j in range(4):
        update(total[:, j * KVW : (j + 1) * KVW], wv, mv, wvb, mvb, (slice(16 * j, 16 * (j + 1)), slice(None)))
    store(mvb, mv_new)
    store(wvb, wv_new)
    for cpy, (_, b, c) in zip(loads[8:], pieces):
        cpy.wait()
        store(b, c)
    for cpy in stores:
        cpy.wait()


def shards(
    value_weight, out_weight, value_moment, out_moment, inputs_saved, queries_saved, keys_saved,
    grad_now, grad_new, bound_now, bound_new,
):
    sections = lax.axis_size("section")
    hbm = pl.BlockSpec(memory_space=pltpu.MemorySpace.HBM)
    dma = pltpu.SemaphoreType.DMA
    gi, dq, dk, fo, fv, ro, rv = pl.pallas_call(
        functools.partial(kernel, sections),
        out_shape=(
            jax.ShapeDtypeStruct((2, 2, TOK, D), bf16),
            jax.ShapeDtypeStruct((2, 2, TOK, QW), bf16),
            jax.ShapeDtypeStruct((2, 2, TOK, KVW), bf16),
            jax.ShapeDtypeStruct((2, TOK, WIDE), f32),
            jax.ShapeDtypeStruct((VROWS, D), f32),
            jax.ShapeDtypeStruct((2, TOK, WIDE), bf16),
            jax.ShapeDtypeStruct((VROWS, D), bf16),
        ),
        in_specs=[hbm] * 9,
        out_specs=(hbm,) * 7,
        scratch_shapes=[
            pltpu.VMEM((2, LANES, ROWS, D), bf16),
            pltpu.VMEM((2, D, KVW), bf16),
            pltpu.VMEM((2, 2, TOK, D), bf16),
            pltpu.VMEM((2, 2, TOK, QW), bf16),
            pltpu.VMEM((2, 2, TOK, KVW), bf16),
            pltpu.VMEM((2, 2, TOK, D), bf16),
            pltpu.VMEM((2, TOK, D), bf16),
            pltpu.VMEM((2, 2, HEADS, TOK, TOK), f32),
            pltpu.VMEM((2, 2, TOK, KVW), bf16),
            pltpu.VMEM((2, HEADS, 2 * TOK, HS), bf16),
            pltpu.VMEM((2, 2, HEADS, TOK, HS), bf16),
            pltpu.VMEM((2, 2, TOK, KVW), bf16),
            pltpu.VMEM((2, 2, TOK, D), bf16),
            pltpu.VMEM((2, 2, TOK, QW), bf16),
            pltpu.VMEM((2, 2, TOK, KVW), bf16),
            pltpu.VMEM((2, 2, TOK, WIDE), bf16),
            pltpu.SMEM((2, sections), jnp.int32),
            pltpu.SMEM((2,), jnp.int32),
            pltpu.VMEM((64, KVW), f32),
            pltpu.VMEM((TOK, D), f32),
            pltpu.VMEM((2, D, KVW), bf16),
            pltpu.VMEM((2, 2, 8, TOK, WIDE), bf16),
            pltpu.VMEM((2, 2, 8, TOK, WIDE), bf16),
            pltpu.VMEM((2, 2, 15, TOK, WIDE), bf16),
            pltpu.VMEM((2, 8, VROWS, D), bf16),
            pltpu.VMEM((2, 8, VROWS, D), bf16),
            pltpu.VMEM((2, 15, VROWS, D), bf16),
            pltpu.VMEM((2, TOK, WIDE), bf16),
            pltpu.VMEM((VROWS, D), bf16),
            pltpu.VMEM((2, TOK, WIDE), f32),
            pltpu.VMEM((VROWS, D), f32),
            pltpu.VMEM((TOK, TOK), f32),
            dma((9,)),
            dma((15,)),
            dma((2,)),
            dma((2, 34)),
            dma((2, 2)),
            dma((2, 2, 21)),
            dma((2,)),
            dma((2, 5)),
            dma((4,)),
            dma((4,)),
            dma((2,)),
            dma((2, 2)),
        ],
        compiler_params=pltpu.CompilerParams(
            collective_id=0, has_side_effects=True, vmem_limit_bytes=64000 * 1024
        ),
    )(
        bound_now[:, :, 0], bound_new[:, 0], value_weight[0], out_weight[0],
        inputs_saved[:, :, 0], queries_saved[:, :, 0], keys_saved[:, :, 0], grad_now[:, 0], grad_new,
    )
    big = jax.ShapeDtypeStruct((TOK, D), f32)
    small = jax.ShapeDtypeStruct((64, KVW), f32)
    gi, dq, dk, wv, wo, mv, mo = pl.pallas_call(
        finish,
        out_shape=(
            jax.ShapeDtypeStruct((2, 2, TOK, D), bf16),
            jax.ShapeDtypeStruct((2, 2, TOK, QW), bf16),
            jax.ShapeDtypeStruct((2, 2, TOK, KVW), bf16),
            small, big, small, big,
        ),
        in_specs=[hbm] * 11,
        out_specs=(hbm,) * 7,
        scratch_shapes=[
            pltpu.VMEM((64, KVW), f32),
            pltpu.VMEM((TOK, D), f32),
            pltpu.VMEM((64, KVW), f32),
            pltpu.VMEM((TOK, D), f32),
            pltpu.VMEM((2, TOK, WIDE), f32),
            pltpu.VMEM((VROWS, D), f32),
            pltpu.VMEM((2, TOK, WIDE), bf16),
            pltpu.VMEM((VROWS, D), bf16),
            pltpu.VMEM((2, 2, TOK, D), bf16),
            pltpu.VMEM((2, 2, TOK, QW), bf16),
            pltpu.VMEM((2, 2, TOK, KVW), bf16),
            pltpu.VMEM((64, KVW), f32),
            pltpu.VMEM((TOK, D), f32),
            pltpu.VMEM((64, KVW), f32),
            pltpu.VMEM((TOK, D), f32),
            dma((15,)),
            dma((11,)),
        ],
        compiler_params=pltpu.CompilerParams(vmem_limit_bytes=64000 * 1024),
    )(value_weight[0], out_weight[0], value_moment[0], out_moment[0], fo, fv, ro, rv, gi, dq, dk)
    return (gi[:, :, None], dq[:, :, None], dk[:, :, None], wv[None], wo[None], mv[None], mo[None])


def solution(mesh):
    return jax.shard_map(
        shards,
        mesh=mesh,
        in_specs=(
            P("section", "lane", None),
            P("section", "lane", None),
            P("section", "lane", None),
            P("section", "lane", None),
            P(None, None, "section", "lane", None),
            P(None, None, "section", "lane", None),
            P(None, None, "section", "lane", None),
            P(None, "section", "lane", None),
            P(None, "lane", None),
            P(None, None, "lane"),
            P(None, "lane"),
        ),
        out_specs=(
            P(None, None, "section", "lane", None),
            P(None, None, "section", "lane", None),
            P(None, None, "section", "lane", None),
            P("section", "lane", None),
            P("section", "lane", None),
            P("section", "lane", None),
            P("section", "lane", None),
        ),
        check_vma=False,
    )
```

```python
import functools
import math

import jax
import jax.numpy as jnp
from jax import lax
from jax.experimental import pallas as pl
from jax.experimental.pallas import tpu as pltpu
from jax.sharding import PartitionSpec as P

TOK = 128
D = 1024
QW = 2048
KVW = 256
HS = 128
HEADS = 16
GROUP = 8
LANES = 16
ROWS = 144
CUT = 80
VROWS = 16
SIDE = 16
UNROLL = 8
HALF = TOK // 2
WIDE = D // 2

decay_rate = 0.9
learn_rate = 0.01
MESH = pl.DeviceIdType.MESH
bf16 = jnp.bfloat16
f32 = jnp.float32

VPLACES = ((2, 1), (1, 1), (3, 1), (0, 1), (2, 0), (1, 0), (3, 0), (0, 0))
PLACES = ((2, 1), (1, 1), (3, 1), (2, 0), (1, 0), (3, 0), (0, 1), (0, 0))


def dot(a, b, dims):
    return lax.dot_general(a, b, (dims, ((), ())), preferred_element_type=f32)


def kernel(
    sections,
    bn_in, bw_in, wv_hbm, wo_hbm, x_hbm, q_hbm, k_hbm, gnow_hbm, gnew_hbm,
    gi_hbm, dq_hbm, dk_hbm, fo_hbm, fv_hbm, mo_hbm, mv_hbm,
    wb, wvs, xs, qs, ks, gs, gnews, pr, vs, at, ga, dvs, gis, dqs, dks, rx,
    bn, bw, wv_in, wo_in, dwv, pc, po, rcn, pcv, pov, rvn, msend, msendv, fin, finv, maskb,
    ld_sem, st_sem, ag_done, ag_recv, rs_done, rs_recv, rv_done, rv_recv, ms_send, ms_recv, nb_done, nb_recv,
):
    s = lax.axis_index("section")
    l = lax.axis_index("lane")
    y = l // 4
    x = (l // 2) % 2
    c = l % 2
    scale = 1.0 / math.sqrt(HS)

    def lane(dy, dx, dc):
        yy = (y + dy) % 4
        xx = (x + dx) % 2
        cc = (c + dc) % 2
        return yy * 4 + xx * 2 + cc

    def slot(q, dy, dx, dc):
        return lane(dy, dx + q, dc)

    xp = (s, lane(0, 1, 0))
    yp = (s, lane(1, 0, 0))
    ym = (s, lane(3, 0, 0))
    cp = (s, lane(0, 0, 1))
    y2 = (s, lane(2, 0, 0))
    mir = (sections - 1 - s, lane(0, 1, 0))
    before = ((s + sections - 1) % sections, l)
    after = ((s + 1) % sections, l)

    barrier = pltpu.get_barrier_semaphore()
    peers = (xp, yp, ym, cp, mir, before, after) + (y2,)
    for p in peers:
        pl.semaphore_signal(barrier, inc=1, device_id=p, device_id_type=MESH)
    loads = [
        pltpu.make_async_copy(wo_hbm, wo_in, ld_sem.at[5]),
        pltpu.make_async_copy(wv_hbm, wv_in, ld_sem.at[6]),
        pltpu.make_async_copy(bn_in, bn, ld_sem.at[7]),
        pltpu.make_async_copy(bw_in, bw, ld_sem.at[8]),
        pltpu.make_async_copy(k_hbm, ks, ld_sem.at[0]),
        pltpu.make_async_copy(q_hbm, qs, ld_sem.at[1]),
        pltpu.make_async_copy(x_hbm, xs, ld_sem.at[2]),
        pltpu.make_async_copy(gnow_hbm, gs.at[:, 0], ld_sem.at[3]),
        pltpu.make_async_copy(gnew_hbm, gnews, ld_sem.at[4]),
    ]
    for cpy in loads:
        cpy.start()
    loads[0].wait()
    loads[1].wait()
    wb[0, l, :TOK, :] = wo_in[...].astype(bf16)
    for j in range(4):
        wb[0, l, TOK:, j * KVW : (j + 1) * KVW] = wv_in[16 * j : 16 * (j + 1), :].astype(bf16)
    pl.semaphore_wait(barrier, len(peers))

    def send(src, dst, ssem, rsem, dev):
        cpy = pltpu.make_async_remote_copy(
            src_ref=src, dst_ref=dst, send_sem=ssem, recv_sem=rsem, device_id=dev, device_id_type=MESH
        )
        cpy.start()

    def arrived(dst, sem):
        pltpu.make_async_copy(dst, dst, sem).wait()

    OWN, X, A, B, OPP, AX, BX, OX = range(8)
    where_is = {
        OWN: (0, 0), X: (0, 1), A: (3, 0), B: (1, 0), OPP: (2, 0), AX: (3, 1), BX: (1, 1), OX: (2, 1),
    }

    def block(q, kind, core=0):
        return wb.at[q, slot(q, *where_is[kind], core)]

    def piece(q, kind, n, core=0):
        return block(q, kind, core).at[pl.ds(0, CUT) if n == 0 else pl.ds(CUT, ROWS - CUT), :]

    def most(q, kind):
        return block(q, kind).at[pl.ds(CUT, TOK - CUT), :]

    def rest(q, kind):
        return block(q, kind).at[pl.ds(TOK, VROWS), :]

    def ag_send(q, kind, n, to, as_kind):
        ref = piece(q, kind, n)
        send(ref, ref, ag_done.at[q], ag_recv.at[q, as_kind * 2 + n], to)

    def ag_send_most(q, kind, to, as_kind):
        ref = most(q, kind)
        send(ref, ref, ag_done.at[q], ag_recv.at[q, as_kind * 2 + 1], to)

    def ag_send_rest(q, kind, as_kind):
        ref = rest(q, kind)
        send(ref, ref, ag_done.at[q], ag_recv.at[q, 32 + as_kind - AX], xp)

    def ag_core(q, kind, n):
        ref = piece(q, kind, n)
        send(ref, ref, ag_done.at[q], ag_recv.at[q, 16 + kind * 2 + n], cp)

    def ag_got(q, kind, n, core=0):
        arrived(piece(q, kind, n, core), ag_recv.at[q, core * 16 + kind * 2 + n])

    def ag_start(q):
        ag_send(q, OWN, 0, yp, A)
        ag_send(q, OWN, 1, ym, B)
        ag_send(q, OWN, 0, xp, X)
        ag_send(q, OWN, 1, yp, A)
        ag_send(q, OWN, 0, ym, B)
        ag_send(q, OWN, 1, xp, X)
        ag_core(q, OWN, 0)
        ag_core(q, OWN, 1)

    def ag_step1(q):
        ag_got(q, A, 0)
        ag_send(q, A, 0, yp, OPP)
        ag_got(q, B, 1)
        ag_send(q, B, 1, ym, OPP)
        ag_core(q, A, 0)
        ag_core(q, B, 1)
        ag_got(q, X, 0)
        ag_send(q, X, 0, yp, AX)
        ag_send(q, X, 0, ym, BX)
        ag_core(q, X, 0)

    def ag_step1b(q):
        ag_got(q, X, 1)
        ag_send_most(q, X, yp, AX)
        ag_send_most(q, X, ym, BX)
        ag_core(q, X, 1)
        ag_got(q, A, 1)
        ag_send_rest(q, A, AX)
        ag_send_rest(q, B, BX)
        ag_core(q, A, 1)
        ag_got(q, B, 0)
        ag_core(q, B, 0)

    def ag_step2(q):
        for n in range(2):
            ag_got(q, OPP, n)
            ag_send(q, OPP, n, xp, OX)
            ag_core(q, OPP, n)

    def ag_step3(q, n):
        for kind in (AX, BX):
            if n == 0:
                ag_got(q, kind, 0)
            else:
                arrived(rest(q, kind), ag_recv.at[q, 32 + kind - AX])
                arrived(most(q, kind), ag_recv.at[q, kind * 2 + 1])
            ag_core(q, kind, n)
        ag_got(q, OX, n)
        ag_core(q, OX, n)

    def grad_attended(q, kinds):
        for kind in kinds:
            ag_got(q, kind, 0, 1)
            ag_got(q, kind, 1, 1)
            n = slot(q, *where_is[kind], 0) // 2
            w2 = jnp.concatenate([wb[q, 2 * n, :TOK, :], wb[q, 2 * n + 1, :TOK, :]], axis=0)
            r = dot(gs[q, 0], w2, ((1,), (1,))).astype(bf16)
            ga[q, 0, 2 * n] = r[:, :HS]
            ga[q, 0, 2 * n + 1] = r[:, HS:]

    def value_rows(q):
        @pl.loop(0, LANES)
        def _(h):
            for j in range(4):
                at_row = pl.multiple_of(h * 64 + 16 * j, 16)
                wvs[q, pl.ds(at_row, 16), :] = wb[q, h, TOK:, j * KVW : (j + 1) * KVW]

    stores = []

    def store(src, dst):
        cpy = pltpu.make_async_copy(src, dst, st_sem.at[len(stores)])
        cpy.start()
        stores.append(cpy)

    def softmax(q, t):
        here = bn[q, s]
        if t == 0:
            bound = here
        elif q == 0:
            bound = jnp.where(s == sections - 1, bw[0], bn[0, jnp.minimum(s + 1, sections - 1)])
        else:
            bound = jnp.where(s == 0, bw[1], bn[1, jnp.maximum(s - 1, 0)])
        row = lax.broadcasted_iota(jnp.int32, (TOK, TOK), 0)
        col = lax.broadcasted_iota(jnp.int32, (TOK, TOK), 1)
        seen = (col <= row) & ((col >= bound) | (row < bound))
        maskb[...] = jnp.where(seen, 0.0, -1e30).astype(f32)
        for g in range(2):
            kg = ks[q, t, :, g * HS : (g + 1) * HS]

            @pl.loop(0, GROUP // UNROLL)
            def _(n):
                for u in range(UNROLL):
                    h = g * GROUP + n * UNROLL + u
                    qh = qs[q, t, :, pl.ds(pl.multiple_of(h * HS, HS), HS)]
                    sc = dot(qh, kg, ((1,), (1,))) * scale + maskb[...]
                    e = jnp.exp(sc - jnp.max(sc, axis=-1, keepdims=True))
                    pr[q, t, h] = e * (1.0 / jnp.sum(e, axis=-1, keepdims=True))

    def values(q):
        for t in range(2):
            vs[q, t] = dot(xs[q, t], wvs[q], ((1,), (0,))).astype(bf16)

    def attended(q, t):
        for g in range(2):
            vg = vs[q, t, :, g * HS : (g + 1) * HS]

            @pl.loop(0, GROUP // 4)
            def _(n):
                for u in range(4):
                    h = g * GROUP + n * 4 + u
                    at[q, h, t * TOK : (t + 1) * TOK, :] = dot(pr[q, t, h].astype(bf16), vg, ((1,), (0,))).astype(bf16)

    def grad_attended_late(q, half):
        @pl.loop(half * HEADS // 4, (half + 1) * HEADS // 4)
        def _(n):
            w2 = jnp.concatenate([wb[q, 2 * n, :TOK, :], wb[q, 2 * n + 1, :TOK, :]], axis=0)
            r = dot(gs[q, 1], w2, ((1,), (1,))).astype(bf16)
            ga[q, 1, 2 * n] = r[:, :HS]
            ga[q, 1, 2 * n + 1] = r[:, HS:]

    def grad_values(q, t):
        for g in range(2):
            p8 = pr[q, t, g * GROUP : (g + 1) * GROUP].astype(bf16).reshape(GROUP * TOK, TOK)
            g8 = ga[q, t, g * GROUP : (g + 1) * GROUP].reshape(GROUP * TOK, HS)
            dvs[q, t, :, g * HS : (g + 1) * HS] = dot(p8, g8, ((0,), (0,))).astype(bf16)
        for n in range(4):
            cols = slice(n * 256, (n + 1) * 256)
            add = dot(dvs[q, t], wvs[q, cols, :], ((1,), (1,)))
            gis[q, t, :, cols] = (gs[q, t, :, cols].astype(f32) + add).astype(bf16)
            if t == 0 and n % 2:
                send(
                    gis.at[q, 0, :, pl.ds(n // 2 * WIDE, WIDE)], rx.at[q, n // 2],
                    nb_done.at[q], nb_recv.at[q, n // 2], before if q == 0 else after,
                )
        store(gis.at[q, t], gi_hbm.at[q, t])

    def take(q, n):
        arrived(rx.at[q, n], nb_recv.at[q, n])
        at_end = s == (sections - 1 if q == 0 else 0)
        cols = slice(n * WIDE, (n + 1) * WIDE)
        gs[q, 1, :, cols] = jnp.where(at_end, gnews[q, :, cols], rx[q, n])

    def score_grads(q, t, only=None):
        for g in range(2) if only is None else (only,):
            kg = ks[q, t, :, g * HS : (g + 1) * HS]
            vg = vs[q, t, :, g * HS : (g + 1) * HS]

            def body(n, acc):
                for u in range(UNROLL):
                    h = g * GROUP + n * UNROLL + u
                    at_col = pl.ds(pl.multiple_of(h * HS, HS), HS)
                    gp = dot(ga[q, t, h], vg, ((1,), (1,)))
                    p = pr[q, t, h]
                    delta = jnp.sum(p * gp, axis=-1, keepdims=True)
                    ds = (p * (gp - delta) * scale).astype(bf16)
                    dqs[q, t, :, at_col] = dot(ds, kg, ((1,), (0,))).astype(bf16)
                    acc = acc + dot(ds, qs[q, t, :, at_col], ((0,), (0,)))
                return acc

            acc = lax.fori_loop(0, GROUP // UNROLL, body, jnp.zeros((TOK, HS), f32))
            dks[q, t, :, g * HS : (g + 1) * HS] = acc.astype(bf16)

    def store_scores(q, t):
        store(dqs.at[q, t], dq_hbm.at[q, t])
        store(dks.at[q, t], dk_hbm.at[q, t])

    def rs_blocks(q, k, places=(0, 1, 2, 3, 4, 5, 6, 7)):
        def one(ref, i, dc):
            r = slot(q, *PLACES[i], dc)
            a = at[q, r]
            gg = gs[q, :, :, k * WIDE : (k + 1) * WIDE].reshape(2 * TOK, WIDE)
            ref[q, k, i] = dot(a, gg, ((0,), (0,))).astype(bf16)

        for i in places:
            one(pc, i, 1)
            send(pc.at[q, k, i], rcn.at[q, k, i], rs_done.at[q, k], rs_recv.at[q, k, 11 + i], cp)
        for i in places:
            one(po, i, 0)

    R1A, R1B, R2A, R2B, R3A, R3B, R4AE, R4AL, R4BE, R4BL, R5 = range(11)
    X2A, X2B = 19, 20
    UP, LOW, ALL = (0, HALF), (HALF, HALF), (0, TOK)
    PLACE_OF = {R1A: 0, R1B: 0, R2A: 1, R2B: 2, R3A: 3, R3B: 3, R4AE: 4, R4AL: 4, R4BE: 5, R4BL: 5, R5: 6, X2A: 1, X2B: 2}
    TOP, BOTTOM = (0, SIDE), (TOK - SIDE, SIDE)
    UNDER, ABOVE = (SIDE, TOK - SIDE), (0, TOK - SIDE)

    def rows_of(ref, rows):
        return ref.at[pl.ds(*rows), :]

    def rs_core(q, k, i):
        arrived(rcn.at[q, k, i], rs_recv.at[q, k, 11 + i])

    def rs_hop(q, k, n, i, to, rows=ALL):
        send(
            rows_of(po.at[q, k, i], rows), rows_of(rcn.at[q, k, 8 + PLACE_OF[n]], rows),
            rs_done.at[q, k], rs_recv.at[q, k, n], to,
        )

    def rs_got(q, k, n, rows=ALL):
        arrived(rows_of(rcn.at[q, k, 8 + PLACE_OF[n]], rows), rs_recv.at[q, k, n])

    def add_in(q, k, i, more, rows=ALL):
        rr = slice(rows[0], rows[0] + rows[1])
        total = po[q, k, i, rr, :].astype(f32) + rcn[q, k, i, rr, :].astype(f32)
        for n in more:
            total = total + rcn[q, k, 8 + PLACE_OF[n], rr, :].astype(f32)
        return total

    def put(q, k, i, more, rows=ALL):
        po[q, k, i, rows[0] : rows[0] + rows[1], :] = add_in(q, k, i, more, rows).astype(bf16)

    def rs_a(q, k):
        rs_core(q, k, 0)
        put(q, k, 0, ())
        rs_hop(q, k, R1A, 0, xp, UP)
        rs_hop(q, k, R1B, 0, xp, LOW)
        rs_core(q, k, 1)
        put(q, k, 1, ())
        rs_hop(q, k, R2A, 1, yp, UNDER)
        rs_core(q, k, 2)
        put(q, k, 2, ())
        rs_hop(q, k, R2B, 2, ym, ABOVE)
        rs_hop(q, k, X2A, 1, xp, TOP)
        rs_hop(q, k, X2B, 2, xp, BOTTOM)

    def rs_early(q, k):
        put(q, k, 4, (), LOW)
        rs_hop(q, k, R4AE, 4, yp, LOW)
        put(q, k, 5, (), UP)
        rs_hop(q, k, R4BE, 5, ym, UP)

    def rs_b(q, k):
        for i in (3, 4, 5):
            rs_core(q, k, i)
        rs_got(q, k, R1A, UP)
        put(q, k, 3, (R1A,), UP)
        rs_hop(q, k, R3A, 3, yp, UP)
        rs_got(q, k, R1B, LOW)
        put(q, k, 3, (R1B,), LOW)
        rs_hop(q, k, R3B, 3, ym, LOW)

    def rs_b2(q, k):
        rs_core(q, k, 6)
        rs_got(q, k, R2A, UNDER)
        rs_got(q, k, R2B, ABOVE)
        put(q, k, 6, (R2B,), TOP)
        put(q, k, 6, (R2A, R2B), (SIDE, TOK - 2 * SIDE))
        put(q, k, 6, (R2A,), BOTTOM)
        rs_hop(q, k, R5, 6, xp)

    def rs_c(q, k):
        rs_got(q, k, X2A, TOP)
        rs_got(q, k, R3A, UP)
        put(q, k, 4, (R3A, X2A), TOP)
        put(q, k, 4, (R3A,), (SIDE, HALF - SIDE))
        rs_hop(q, k, R4AL, 4, yp, UP)
        rs_got(q, k, X2B, BOTTOM)
        rs_got(q, k, R3B, LOW)
        put(q, k, 5, (R3B,), (HALF, HALF - SIDE))
        put(q, k, 5, (R3B, X2B), BOTTOM)
        rs_hop(q, k, R4BL, 5, ym, LOW)


    def rv_start(q):
        xt = xs[q].reshape(2 * TOK, D)
        dv = dvs[q].reshape(2 * TOK, KVW)
        for n in range(4):
            dwv[q, n * 256 : (n + 1) * 256, :] = dot(xt[:, n * 256 : (n + 1) * 256], dv, ((0,), (0,))).astype(bf16)
        for ref, dc in ((pcv, 1), (pov, 0)):
            for i in range(8):
                r = slot(q, *VPLACES[i], dc)
                for j in range(4):
                    at_row = pl.multiple_of(r * 64 + 16 * j, 16)
                    ref[q, i, :, j * KVW : (j + 1) * KVW] = dwv[q, pl.ds(at_row, 16), :]
            if dc == 1:
                send(pcv.at[q], rvn.at[q, pl.ds(0, 8)], rv_done.at[q], rv_recv.at[q, 0], cp)

    def rv_a(q):
        arrived(rvn.at[q, pl.ds(0, 8)], rv_recv.at[q, 0])
        for i in range(8):
            pov[q, i] = (pov[q, i].astype(f32) + rvn[q, i].astype(f32)).astype(bf16)
        send(pov.at[q, pl.ds(0, 4)], rvn.at[q, pl.ds(8, 4)], rv_done.at[q], rv_recv.at[q, 1], xp)

    def rv_b(q):
        arrived(rvn.at[q, pl.ds(8, 4)], rv_recv.at[q, 1])
        for i in range(4):
            pov[q, 4 + i] = (pov[q, 4 + i].astype(f32) + rvn[q, 8 + i].astype(f32)).astype(bf16)
        for i, to in ((0, y2), (1, yp), (2, ym)):
            send(pov.at[q, 4 + i], rvn.at[q, 12 + i], rv_done.at[q], rv_recv.at[q, 2 + i], to)

    def rv_final(q):
        total = pov[q, 7].astype(f32)
        for i in range(3):
            arrived(rvn.at[q, 12 + i], rv_recv.at[q, 2 + i])
            total = total + rvn[q, 12 + i].astype(f32)
        if q == 0:
            finv[...] = total
            store(finv, fv_hbm)
        else:
            msendv[...] = total.astype(bf16)
            send(msendv, mv_hbm, ms_send.at[3], ms_recv.at[3], mir)

    def rs_final(q, k):
        rs_core(q, k, 7)
        rs_got(q, k, R5)
        rs_got(q, k, R4AE, LOW)
        rs_got(q, k, R4BE, UP)
        rs_got(q, k, R4AL, UP)
        rs_got(q, k, R4BL, LOW)
        for rows in (UP, LOW):
            total = add_in(q, k, 7, (R4AL, R4BL, R5), rows)
            here = slice(rows[0], rows[0] + rows[1])
            if q == 0:
                fin[k, here, :] = total
            else:
                msend[k, here, :] = total.astype(bf16)
        if q == 0:
            store(fin.at[k], fo_hbm.at[k])
        else:
            send(msend.at[k], mo_hbm.at[k], ms_send.at[1 + k], ms_recv.at[1 + k], mir)

    own = block(0, OWN)
    ag_start(0)
    send(own, wb.at[1, l], ms_send.at[0], ms_recv.at[0], mir)
    for cpy in loads[2:6]:
        cpy.wait()
    softmax(0, 0)
    softmax(0, 1)
    ag_step1(0)
    softmax(1, 0)
    ag_step1b(0)
    softmax(1, 1)
    ag_step2(0)
    for cpy in loads[6:]:
        cpy.wait()
    grad_attended(0, (OWN, A, B, X))
    arrived(block(1, OWN), ms_recv.at[0])
    ag_start(1)
    ag_step3(0, 0)
    grad_attended(0, (OPP,))
    ag_step3(0, 1)
    ag_step1(1)
    grad_attended(0, (AX, BX, OX))
    value_rows(0)
    grad_values(0, 0)
    values(0)
    attended(0, 0)
    ag_step1b(1)
    attended(0, 1)
    ag_step2(1)
    take(0, 0)
    rs_blocks(0, 0)
    rs_a(0, 0)
    grad_attended(1, (OWN, A, B, X))
    ag_step3(1, 0)
    take(0, 1)
    rs_blocks(0, 1)
    ag_step3(1, 1)
    rs_a(0, 1)
    grad_attended(1, (OPP,))
    grad_attended_late(0, 0)
    grad_attended(1, (AX, BX, OX))
    value_rows(1)
    grad_values(1, 0)
    rs_b(0, 0)
    rs_early(0, 0)
    rs_b2(0, 0)
    values(1)
    attended(1, 0)
    rs_b(0, 1)
    grad_attended_late(0, 1)
    grad_values(0, 1)
    rv_start(0)
    rs_c(0, 0)
    attended(1, 1)
    rv_a(0)
    take(1, 0)
    rs_blocks(1, 0)
    rs_a(1, 0)
    take(1, 1)
    rs_blocks(1, 1)
    rs_a(1, 1)
    grad_attended_late(1, 0)
    rs_b(1, 0)
    grad_attended_late(1, 1)
    grad_values(1, 1)
    rv_start(1)
    rs_b2(1, 0)
    rs_b(1, 1)
    rs_early(1, 0)
    rs_c(1, 0)
    rv_a(1)
    rs_b2(1, 1)
    rs_early(1, 1)
    rs_c(1, 1)
    rs_b2(0, 1)
    score_grads(0, 0, 0)
    rs_final(1, 0)
    rv_b(1)
    rs_early(0, 1)
    rs_c(0, 1)
    rv_b(0)
    score_grads(0, 0, 1)
    store_scores(0, 0)
    score_grads(1, 0, 0)
    rs_final(1, 1)
    rv_final(1)
    score_grads(1, 0, 1)
    store_scores(1, 0)
    score_grads(1, 1)
    store_scores(1, 1)
    rs_final(0, 0)
    score_grads(0, 1)
    store_scores(0, 1)
    rs_final(0, 1)
    rv_final(0)
    def ending():
        for n in range(2):
            arrived(mo_hbm.at[n], ms_recv.at[1 + n])
        arrived(mv_hbm, ms_recv.at[3])

    def settle():
        for cpy in stores:
            cpy.wait()

    def leave():
        for q in range(2):
            arrived(wb.at[q, pl.ds(0, 15)], ag_done.at[q])
            for k in range(2):
                arrived(rcn.at[q, k], rs_done.at[q, k])
            arrived(rvn.at[q], rv_done.at[q])
            arrived(rx.at[q], nb_done.at[q])
        arrived(wb.at[1, 0], ms_send.at[0])
        for n in range(2):
            arrived(msend.at[n], ms_send.at[1 + n])
        arrived(msendv, ms_send.at[3])

    ending()
    settle()
    leave()


def finish(
    wv_in, wo_in, mv_in, mo_in, fo_in, fv_in, ro_in, rv_in, gi_in, dq_in, dk_in,
    gi, dq, dk, wv_new, wo_new, mv_new, mo_new,
    wv, wo, mv, mo, fo, fv, ro, rv, gib, dqb, dkb, wvb, wob, mvb, mob, in_sem, out_sem,
):
    firsts = [(fo_in, fo), (ro_in, ro), (wo_in, wo), (mo_in, mo), (fv_in, fv), (rv_in, rv), (wv_in, wv), (mv_in, mv)]
    pieces = [(dq_in.at[q, t], dqb.at[q, t], dq.at[q, t]) for q in range(2) for t in range(2)]
    pieces += [(gi_in.at[q], gib.at[q], gi.at[q]) for q in range(2)]
    pieces += [(dk_in, dkb, dk)]
    loads = [pltpu.make_async_copy(a, b, in_sem.at[n]) for n, (a, b, *_) in enumerate(firsts + pieces)]
    for cpy in loads:
        cpy.start()
    stores = []

    def store(src, dst):
        cpy = pltpu.make_async_copy(src, dst, out_sem.at[len(stores)])
        cpy.start()
        stores.append(cpy)

    for cpy in loads[:8]:
        cpy.wait()

    def update(total, w, m, w_buf, m_buf, at):
        moment = decay_rate * m[at] + total / LANES
        m_buf[at] = moment
        w_buf[at] = w[at] - learn_rate * moment

    for n in range(2):
        update(fo[n] + ro[n].astype(f32), wo, mo, wob, mob, (slice(None), slice(n * WIDE, (n + 1) * WIDE)))
    store(mob, mo_new)
    store(wob, wo_new)
    total = fv[...] + rv[...].astype(f32)
    for j in range(4):
        update(total[:, j * KVW : (j + 1) * KVW], wv, mv, wvb, mvb, (slice(16 * j, 16 * (j + 1)), slice(None)))
    store(mvb, mv_new)
    store(wvb, wv_new)
    for cpy, (_, b, c) in zip(loads[8:], pieces):
        cpy.wait()
        store(b, c)
    for cpy in stores:
        cpy.wait()


def shards(
    value_weight, out_weight, value_moment, out_moment, inputs_saved, queries_saved, keys_saved,
    grad_now, grad_new, bound_now, bound_new,
):
    sections = lax.axis_size("section")
    hbm = pl.BlockSpec(memory_space=pltpu.MemorySpace.HBM)
    dma = pltpu.SemaphoreType.DMA
    gi, dq, dk, fo, fv, ro, rv = pl.pallas_call(
        functools.partial(kernel, sections),
        out_shape=(
            jax.ShapeDtypeStruct((2, 2, TOK, D), bf16),
            jax.ShapeDtypeStruct((2, 2, TOK, QW), bf16),
            jax.ShapeDtypeStruct((2, 2, TOK, KVW), bf16),
            jax.ShapeDtypeStruct((2, TOK, WIDE), f32),
            jax.ShapeDtypeStruct((VROWS, D), f32),
            jax.ShapeDtypeStruct((2, TOK, WIDE), bf16),
            jax.ShapeDtypeStruct((VROWS, D), bf16),
        ),
        in_specs=[hbm] * 9,
        out_specs=(hbm,) * 7,
        scratch_shapes=[
            pltpu.VMEM((2, LANES, ROWS, D), bf16),
            pltpu.VMEM((2, D, KVW), bf16),
            pltpu.VMEM((2, 2, TOK, D), bf16),
            pltpu.VMEM((2, 2, TOK, QW), bf16),
            pltpu.VMEM((2, 2, TOK, KVW), bf16),
            pltpu.VMEM((2, 2, TOK, D), bf16),
            pltpu.VMEM((2, TOK, D), bf16),
            pltpu.VMEM((2, 2, HEADS, TOK, TOK), f32),
            pltpu.VMEM((2, 2, TOK, KVW), bf16),
            pltpu.VMEM((2, HEADS, 2 * TOK, HS), bf16),
            pltpu.VMEM((2, 2, HEADS, TOK, HS), bf16),
            pltpu.VMEM((2, 2, TOK, KVW), bf16),
            pltpu.VMEM((2, 2, TOK, D), bf16),
            pltpu.VMEM((2, 2, TOK, QW), bf16),
            pltpu.VMEM((2, 2, TOK, KVW), bf16),
            pltpu.VMEM((2, 2, TOK, WIDE), bf16),
            pltpu.SMEM((2, sections), jnp.int32),
            pltpu.SMEM((2,), jnp.int32),
            pltpu.VMEM((64, KVW), f32),
            pltpu.VMEM((TOK, D), f32),
            pltpu.VMEM((2, D, KVW), bf16),
            pltpu.VMEM((2, 2, 8, TOK, WIDE), bf16),
            pltpu.VMEM((2, 2, 8, TOK, WIDE), bf16),
            pltpu.VMEM((2, 2, 15, TOK, WIDE), bf16),
            pltpu.VMEM((2, 8, VROWS, D), bf16),
            pltpu.VMEM((2, 8, VROWS, D), bf16),
            pltpu.VMEM((2, 15, VROWS, D), bf16),
            pltpu.VMEM((2, TOK, WIDE), bf16),
            pltpu.VMEM((VROWS, D), bf16),
            pltpu.VMEM((2, TOK, WIDE), f32),
            pltpu.VMEM((VROWS, D), f32),
            pltpu.VMEM((TOK, TOK), f32),
            dma((9,)),
            dma((15,)),
            dma((2,)),
            dma((2, 34)),
            dma((2, 2)),
            dma((2, 2, 21)),
            dma((2,)),
            dma((2, 5)),
            dma((4,)),
            dma((4,)),
            dma((2,)),
            dma((2, 2)),
        ],
        compiler_params=pltpu.CompilerParams(
            collective_id=0, has_side_effects=True, vmem_limit_bytes=64000 * 1024
        ),
    )(
        bound_now[:, :, 0], bound_new[:, 0], value_weight[0], out_weight[0],
        inputs_saved[:, :, 0], queries_saved[:, :, 0], keys_saved[:, :, 0], grad_now[:, 0], grad_new,
    )
    big = jax.ShapeDtypeStruct((TOK, D), f32)
    small = jax.ShapeDtypeStruct((64, KVW), f32)
    gi, dq, dk, wv, wo, mv, mo = pl.pallas_call(
        finish,
        out_shape=(
            jax.ShapeDtypeStruct((2, 2, TOK, D), bf16),
            jax.ShapeDtypeStruct((2, 2, TOK, QW), bf16),
            jax.ShapeDtypeStruct((2, 2, TOK, KVW), bf16),
            small, big, small, big,
        ),
        in_specs=[hbm] * 11,
        out_specs=(hbm,) * 7,
        scratch_shapes=[
            pltpu.VMEM((64, KVW), f32),
            pltpu.VMEM((TOK, D), f32),
            pltpu.VMEM((64, KVW), f32),
            pltpu.VMEM((TOK, D), f32),
            pltpu.VMEM((2, TOK, WIDE), f32),
            pltpu.VMEM((VROWS, D), f32),
            pltpu.VMEM((2, TOK, WIDE), bf16),
            pltpu.VMEM((VROWS, D), bf16),
            pltpu.VMEM((2, 2, TOK, D), bf16),
            pltpu.VMEM((2, 2, TOK, QW), bf16),
            pltpu.VMEM((2, 2, TOK, KVW), bf16),
            pltpu.VMEM((64, KVW), f32),
            pltpu.VMEM((TOK, D), f32),
            pltpu.VMEM((64, KVW), f32),
            pltpu.VMEM((TOK, D), f32),
            dma((15,)),
            dma((11,)),
        ],
        compiler_params=pltpu.CompilerParams(vmem_limit_bytes=64000 * 1024),
    )(value_weight[0], out_weight[0], value_moment[0], out_moment[0], fo, fv, ro, rv, gi, dq, dk)
    return (gi[:, :, None], dq[:, :, None], dk[:, :, None], wv[None], wo[None], mv[None], mo[None])


def solution(mesh):
    return jax.shard_map(
        shards,
        mesh=mesh,
        in_specs=(
            P("section", "lane", None),
            P("section", "lane", None),
            P("section", "lane", None),
            P("section", "lane", None),
            P(None, None, "section", "lane", None),
            P(None, None, "section", "lane", None),
            P(None, None, "section", "lane", None),
            P(None, "section", "lane", None),
            P(None, "lane", None),
            P(None, None, "lane"),
            P(None, "lane"),
        ),
        out_specs=(
            P(None, None, "section", "lane", None),
            P(None, None, "section", "lane", None),
            P(None, None, "section", "lane", None),
            P("section", "lane", None),
            P("section", "lane", None),
            P("section", "lane", None),
            P("section", "lane", None),
        ),
        check_vma=False,
    )
```
